128 devices in a mesh: req: 8 (over y, z_hi), mlp: 16 (over z_lo, x, core).
Axes of the slice: x: 4, y: 4, z: 4 (z_hi: 2, z_lo: 2; z = z_hi * 2 + z_lo), core: 2. Of those that a mesh axis runs over, the one named last changes fastest.
Arguments:
- prompt_tokens: bfloat16 [16, 1024, 2048], P('req', None, 'mlp'), may hold values from -6 to 6
- decode_tokens: bfloat16 [32, 2048], P('req', 'mlp'), may hold values from -6 to 6
- prompt_lengths: int32 [16], P('req'), may hold values from 128 to 1024, as said below
- decode_states: float32 [32, 16, 128, 128], P('req', 'mlp'), may hold values from -6 to 6
- w_fio: float32 [2048, 6144], P('req', 'mlp'), may hold values from -0.125 to 0.125
- forget_bias: float32 [2048], P('mlp'), as said below
- head_gain: float32 [2048], P('mlp'), may hold values from 0.1 to 1.9
- w_out: float32 [2048, 2048], P('mlp', 'req'), may hold values from -0.125 to 0.125
- mlp_gain: float32 [2048], replicated, may hold values from 0.1 to 1.9
- w_gu: float32 [2048, 11264], P('req', 'mlp'), may hold values from -0.125 to 0.125
- w_down: float32 [5632, 2048], P('mlp', 'req'), may hold values from -0.078125 to 0.078125
Outputs:
- prompt_out: bfloat16 [16, 1024, 2048], P('req', None, 'mlp')
- decode_out: bfloat16 [32, 2048], P('req', 'mlp')
- prompt_states: float32 [16, 16, 128, 128], P('req', 'mlp')
- decode_next: float32 [32, 16, 128, 128], P('req', 'mlp')
The draws below stay inside these ranges and needn't reach their ends.
Inputs may be any that keep to these rules, and one draw needn't show every extreme that they name: `prompt_lengths`: slots at or past a prompt's length are padding; one prompt has length 1024 and another 1024 // 8. `forget_bias`: every entry is at least 3 and at most ln(1024) + 1.7.
All inputs are finite; a program needn't handle non-finite values.
Results may differ from the reference program's by a relative error of at most 0.02.
Values may be sent and summed in bfloat16 or wider, within the bound.
No kernel may reach another device: no remote copies, remote signals or barrier semaphores. Data moves between devices by JAX's collectives and lax.ppermute only.
A program may use at most 128 MiB of HBM per device.

```python
import jax
import jax.numpy as jnp
from jax import lax

D = 2048
H = 16
DK = 128
FF = 5632
PLEN = 1024
PROMPTS = 16
DECODES = 32
FF_DEV = 352
N_MLP = 16


def draw_prompt_lengths(key, part):
    first_key = jax.random.fold_in(key, 11)
    second_key = jax.random.fold_in(key, 12)
    drawn = jax.random.randint(first_key, (PROMPTS,), PLEN // 8, PLEN + 1)
    chosen = jax.random.randint(second_key, (), 0, PROMPTS)
    indices = jnp.arange(PROMPTS, dtype=jnp.int32)
    drawn = jnp.where(indices == chosen, PLEN, drawn)
    drawn = jnp.where(indices == (chosen + 1) % PROMPTS, PLEN // 8, drawn)
    return drawn.astype(jnp.int32)


def draw_forget_bias(key, part):
    first_key = jax.random.fold_in(key, 21)
    second_key = jax.random.fold_in(key, 22)
    slow_heads = jax.random.randint(first_key, (H, 1), 0, 2)
    spread = jax.random.uniform(second_key, (H, DK), jnp.float32, 0.0, 1.0)
    slow_value = jnp.log(jnp.float32(PLEN)) + 0.7 + spread
    fast_value = 3.0 + spread
    return jnp.where(slow_heads == 1, slow_value, fast_value).reshape(H * DK).astype(jnp.float32)


def block_scale(rng, shape, cuts, low, high):
    factor_of = 1.0
    for dim, parts in cuts:
        draws = jax.random.uniform(jax.random.fold_in(jax.random.fold_in(rng, 6), dim), (parts,), jnp.float32, low / len(cuts), high / len(cuts))
        factor_of = factor_of * jnp.repeat(jnp.exp(draws), shape[dim] // parts).reshape((-1,) + (1,) * (len(shape) - 1 - dim))
    return factor_of


def gaussian(own_key, extent, width, reach, shards=(), kind=jnp.bfloat16):
    factor_of = block_scale(own_key, extent, shards, -0.22, 0.18) if shards else 1.0
    result = jax.random.normal(own_key, extent, jnp.float32) * width * factor_of
    return jnp.minimum(jnp.maximum(result, -reach), reach).astype(kind)


def setup_inputs(seed: int = 0) -> dict:
    arg_keys = jax.random.split(jax.random.key(seed), 12)
    prompt_tokens = gaussian(arg_keys[0], (PROMPTS, PLEN, D), 1.0, 6.0, ((0, 8), (2, 16)))
    decode_tokens = gaussian(arg_keys[1], (DECODES, D), 1.0, 6.0, ((0, 8), (1, 16)))
    prompt_lengths = draw_prompt_lengths(jax.random.fold_in(arg_keys[11], 71), 0)
    decode_states = gaussian(arg_keys[3], (DECODES, H, DK, DK), 1.0, 6.0, ((0, 8), (1, 16)), jnp.float32)
    w_fio = gaussian(arg_keys[4], (D, 3 * H * DK), D ** -0.5, 0.125, ((0, 8), (1, 16)), jnp.float32)
    forget_bias = draw_forget_bias(jax.random.fold_in(arg_keys[11], 71), 0)
    head_gain = jnp.clip(1.0 + 0.18 * jax.random.normal(arg_keys[6], (H * DK,), jnp.float32), 0.1, 1.9)
    w_out = gaussian(arg_keys[7], (H * DK, D), (H * DK) ** -0.5, 0.125, ((0, 16), (1, 8)), jnp.float32)
    mlp_gain = jnp.clip(1.0 + 0.18 * jax.random.normal(arg_keys[8], (D,), jnp.float32), 0.1, 1.9)
    w_gu = gaussian(arg_keys[9], (D, 2 * FF), D ** -0.5, 0.125, ((0, 8), (1, 16)), jnp.float32)
    w_down = gaussian(arg_keys[10], (FF, D), FF ** -0.5, 0.078125, ((0, 16), (1, 8)), jnp.float32)
    return {"prompt_tokens": prompt_tokens, "decode_tokens": decode_tokens, "prompt_lengths": prompt_lengths, "decode_states": decode_states, "w_fio": w_fio, "forget_bias": forget_bias, "head_gain": head_gain, "w_out": w_out, "mlp_gain": mlp_gain, "w_gu": w_gu, "w_down": w_down}


epsilon = 1e-05

def head_norm(source_rows, scales):
    mean_square = lax.optimization_barrier(jnp.mean(source_rows * source_rows, axis=-1, keepdims=True))
    return source_rows * lax.rsqrt(mean_square + epsilon) * scales

def reference(prompt_tokens, decode_tokens, prompt_lengths, decode_states, w_fio, forget_bias, head_gain, w_out, mlp_gain, w_gu, w_down):
    prompt_rows = PROMPTS * PLEN
    x_rows = jnp.concatenate([prompt_tokens.reshape(prompt_rows, D), decode_tokens], axis=0)
    mixing = jnp.dot(x_rows, w_fio.astype(jnp.bfloat16), preferred_element_type=jnp.float32)
    mixing = mixing.reshape(-1, H, 3, DK)
    bias_table = forget_bias.reshape(H, DK)
    forget_logit = mixing[:, :, 0] + bias_table
    values = mixing[:, :, 1]
    queries = mixing[:, :, 2]

    def time_first(source_array):
        return source_array[:prompt_rows].reshape(PROMPTS, PLEN, H, DK).transpose(1, 0, 2, 3)
    alive_mask = jnp.arange(PLEN, dtype=jnp.int32)[:, None] < prompt_lengths[None, :]

    def advance(carried, inputs):
        forget_now, value_now, query_now, alive_now = inputs
        alive_wide = alive_now[:, None, None]
        forget_gate = jnp.where(alive_wide, jax.nn.sigmoid(forget_now), 1.0)
        key_gate = jnp.where(alive_wide, jax.nn.sigmoid(-forget_now), 0.0)
        carried = forget_gate[..., None] * carried + key_gate[..., None] * value_now[:, :, None, :]
        emitted = jnp.einsum('phcv,phc->phv', carried, query_now, precision=lax.Precision.HIGHEST)
        emitted = jnp.where(alive_wide, emitted, 0.0)
        return (carried, emitted)
    start_state = jnp.zeros((PROMPTS, H, DK, DK), jnp.float32)
    prompt_states, prompt_mixed = lax.scan(advance, start_state, (time_first(forget_logit), time_first(values), time_first(queries), alive_mask))
    prompt_mixed = prompt_mixed.transpose(1, 0, 2, 3).reshape(prompt_rows, H, DK)
    decode_logit = forget_logit[prompt_rows:]
    decode_next = jax.nn.sigmoid(decode_logit)[..., None] * decode_states + jax.nn.sigmoid(-decode_logit)[..., None] * values[prompt_rows:][:, :, None, :]
    decode_mixed = jnp.einsum('nhcv,nhc->nhv', decode_next, queries[prompt_rows:], precision=lax.Precision.HIGHEST)
    mixed_all = jnp.concatenate([prompt_mixed, decode_mixed], axis=0)
    head_rows = head_norm(mixed_all, head_gain.reshape(H, DK)).astype(jnp.bfloat16).reshape(-1, H * DK)
    attention = jnp.dot(head_rows, w_out.astype(jnp.bfloat16), preferred_element_type=jnp.float32)
    residual = (x_rows.astype(jnp.float32) + attention).astype(jnp.bfloat16)
    residual_wide = residual.astype(jnp.float32)
    normed = (head_norm(residual_wide, 1.0) * mlp_gain).astype(jnp.bfloat16)
    gate_up = jnp.dot(normed, w_gu.astype(jnp.bfloat16), preferred_element_type=jnp.float32)
    gate_up = gate_up.reshape(-1, N_MLP, 2, FF_DEV)
    gate_part = gate_up[:, :, 0].reshape(-1, FF)
    up_part = gate_up[:, :, 1].reshape(-1, FF)
    hidden = (jax.nn.silu(gate_part) * up_part).astype(jnp.bfloat16)
    total_rows = hidden.shape[0]
    hidden_blocks = hidden.reshape(total_rows, N_MLP, FF_DEV).transpose(1, 0, 2)
    down_blocks = w_down.astype(jnp.bfloat16).reshape(N_MLP, FF_DEV, D)

    def add_block(running, pair):
        hidden_block, down_block = pair
        part_sum = jnp.dot(hidden_block, down_block, preferred_element_type=jnp.float32).astype(jnp.bfloat16)
        part_sum = lax.optimization_barrier(part_sum)
        return (running + part_sum.astype(jnp.float32), None)
    down_total, unused = lax.scan(add_block, jnp.zeros((total_rows, D), jnp.float32), (hidden_blocks, down_blocks))
    layer_output = (residual_wide + down_total).astype(jnp.bfloat16)
    return (layer_output[:prompt_rows].reshape(PROMPTS, PLEN, D), layer_output[prompt_rows:], prompt_states, decode_next)
```

```python
import functools

import jax
import jax.numpy as jnp
import numpy as np
from jax import lax
from jax.experimental import pallas as pl
from jax.experimental.pallas import tpu as pltpu
from jax.sharding import Mesh, PartitionSpec as P

EPS = 1e-5
HALF = 528
CH = 128
LEVELS = 7
BF = jnp.bfloat16
F32 = jnp.float32
SIZES = {"y": 4, "zh": 2, "zl": 2, "x": 4, "c": 2}
VMEM_LIMIT = 60 * 1024 * 1024


def shift(value, axis, step):
    n = SIZES[axis]
    return lax.ppermute(value, axis, [(i, (i + step) % n) for i in range(n)])


def ring_gather(own, axis):
    n = own.shape[0] // 2
    before = shift(own, axis, 1)
    ahead = shift(own, axis, -1)
    far0 = shift(before[:n], axis, 1)
    far1 = shift(ahead[n:], axis, -1)
    return [own, ahead, far0, far1, before]


def piece(refs, step, part, parts=2):
    if step == 2:
        n = parts // 2
        return refs[2 + part // n].at[part % n]
    return refs[{0: 0, 1: 1, 3: 4}[step]].at[part]


def weight_blocks(refs, idx):
    y, z = idx[0], idx[1] * 2 + idx[2]
    for k in range(4):
        for j in range(4):
            r = 2 * ((y + k) & 3) + (((z + j) & 3) >> 1)
            yield piece(refs, k, j, 4), j & 1, r


def level_matrix():
    t = np.arange(CH)[:, None]
    u = np.arange(CH)[None, :]
    rows = []
    for level in range(LEVELS):
        b = 1 << level
        ref = (t // (2 * b)) * 2 * b + b - 1
        late = (t % (2 * b)) >= b
        rows.append(np.where(late, (u > ref) & (u <= t), (u > t) & (u <= ref)))
    rows.append(u <= t)
    rows.append(u > t)
    return np.concatenate(rows, 0).astype(np.float32)


def dot_nt(a, b):
    return lax.dot_general(a, b, (((1,), (1,)), ((), ())), preferred_element_type=F32)


def dot_tn(a, b):
    return lax.dot_general(a, b, (((0,), (0,)), ((), ())), preferred_element_type=F32)


def dot_nn(a, b):
    return jnp.dot(a, b, preferred_element_type=F32)


def copy_all(copies, sems):
    started = []
    for i, (src, dst) in enumerate(copies):
        cp = pltpu.make_async_copy(src, dst, sems.at[i])
        cp.start()
        started.append(cp)
    return started


def col(r):
    return pl.ds(pl.multiple_of(r * 256, 256), 256)


def x_copies(refs, cat, x):
    out = []
    for k in range(4):
        for z in range(2):
            r = z * 4 + ((x + k) & 3)
            out.append((piece(refs, k, z), cat.at[:, col(r)]))
    return out


def head_out(o, gain):
    ms = jnp.mean(o * o, axis=-1, keepdims=True)
    return o * lax.rsqrt(ms + EPS) * gain


def mix_kernel(
    idx, xo0, xo1, xo2, xo3, xo4, xp0, xp1, xp2, xp3, xp4, w0, w1, w2, w3, w4,
    bias_ref, gain_ref, mat_ref, dst_ref,
    own_ref, other_ref, state_ref,
    xcat, wcat, mix, oscr, carry, sems,
):
    x, c, length = idx[3], idx[4], idx[5]
    copies = x_copies((xo0, xo1, xo2, xo3, xo4), xcat.at[0], x)
    copies += x_copies((xp0, xp1, xp2, xp3, xp4), xcat.at[1], x)
    for ref, j, r in weight_blocks((w0, w1, w2, w3, w4), idx):
        copies.append((ref, wcat.at[j * 384 : (j + 1) * 384, col(r)]))
    for cp in copy_all(copies, sems):
        cp.wait()
    for hr in range(2):
        ha = (c + hr) & 1

        def project(i, unused, hr=hr, ha=ha):
            rows = pl.ds(pl.multiple_of(i * 176, 16), 176)
            mix[ha, rows, :] = dot_nt(xcat[hr, rows, :], wcat[...])
            return unused

        lax.fori_loop(0, 3, project, 0)
    carry[...] = jnp.zeros_like(carry)
    t = lax.broadcasted_iota(jnp.int32, (CH, CH), 0)
    s = lax.broadcasted_iota(jnp.int32, (CH, CH), 1)
    pair = jnp.where(t > s, t ^ s, 0)
    diag = t == s
    row = lax.broadcasted_iota(jnp.int32, (CH, 128), 0)

    def chunk(n, unused):
        h = n // 4
        rows = pl.ds(pl.multiple_of((n % 4) * CH, CH), CH)
        alive = (row + n * CH) < length
        for j in range(2):
            z = mix[h, rows, j * 384 : j * 384 + 128] + bias_ref[j : j + 1, :]
            v = mix[h, rows, j * 384 + 128 : j * 384 + 256].astype(BF)
            q = mix[h, rows, j * 384 + 256 : j * 384 + 384]
            e = jnp.exp(-jnp.abs(z))
            logf = jnp.where(alive, jnp.minimum(z, 0.0) - jnp.log1p(e), 0.0)
            inv = 1.0 / (1.0 + e)
            k = jnp.where(alive, jnp.where(z >= 0, e * inv, inv), 0.0)
            hi = logf.astype(BF)
            lo = (logf - hi.astype(F32)).astype(BF)
            d = dot_nn(mat_ref[...], jnp.concatenate([hi, lo], axis=1))
            decay = jnp.exp(d[:, :128] + d[:, 128:])
            scores = jnp.where(diag, dot_nt(q.astype(BF), k.astype(BF)), 0.0)
            for level in range(LEVELS):
                el = decay[level * CH : (level + 1) * CH]
                part = dot_nt((q * el).astype(BF), (k * el).astype(BF))
                scores = jnp.where((pair >> level) == 1, part, scores)
            es = decay[LEVELS * CH : (LEVELS + 1) * CH]
            ee = decay[(LEVELS + 1) * CH :]
            held = carry[j]
            o = dot_nn(scores.astype(BF), v) + dot_nt((q * es).astype(BF), held.astype(BF))
            o = jnp.where(alive, o, 0.0)
            carry[j] = held * es[CH - 1 :, :] + dot_tn(v, (k * ee).astype(BF))
            oscr[h, rows, j * 128 : (j + 1) * 128] = head_out(o, gain_ref[j : j + 1, :]).astype(BF)
        return unused

    lax.fori_loop(0, 8, chunk, 0)
    first = lax.broadcasted_iota(jnp.int32, (16, 128), 0) == 0
    for h in range(2):
        for j in range(2):
            z = mix[h, 512:513, j * 384 : j * 384 + 128] + bias_ref[j : j + 1, :]
            v = mix[h, 512:513, j * 384 + 128 : j * 384 + 256]
            q = mix[h, 512:513, j * 384 + 256 : j * 384 + 384]
            e = jnp.exp(-jnp.abs(z))
            inv = 1.0 / (1.0 + e)
            f = jnp.where(z >= 0, inv, e * inv)
            k = jnp.where(z >= 0, e * inv, inv)
            ft = jnp.broadcast_to(f, (128, 128)).T
            kt = jnp.broadcast_to(k, (128, 128)).T
            qt = jnp.broadcast_to(q, (128, 128)).T
            nxt = ft * dst_ref[j, h] + kt * v
            state_ref[j, h] = nxt
            o = head_out(jnp.sum(nxt * qt, axis=0, keepdims=True), gain_ref[j : j + 1, :])
            wide = jnp.where(first, jnp.broadcast_to(o, (16, 128)), 0.0)
            oscr[h, 512:528, j * 128 : (j + 1) * 128] = wide.astype(BF)
    for j in range(2):
        state_ref[j, 2] = carry[j].T
    own_ref[...] = oscr[c]
    other_ref[...] = oscr[1 - c]


def anyspec():
    return pl.BlockSpec(memory_space=pl.ANY)


def vspec():
    return pl.BlockSpec(memory_space=pltpu.VMEM)


def sspec():
    return pl.BlockSpec(memory_space=pltpu.SMEM)


def mix_call(idx, xo, xp, w, bias, gain, dst):
    mat = jnp.asarray(level_matrix(), BF)
    return pl.pallas_call(
        mix_kernel,
        out_shape=(
            jax.ShapeDtypeStruct((HALF, 256), BF),
            jax.ShapeDtypeStruct((HALF, 256), BF),
            jax.ShapeDtypeStruct((2, 3, 128, 128), F32),
        ),
        in_specs=[sspec()] + [anyspec()] * 15 + [vspec()] * 4,
        out_specs=(vspec(),) * 3,
        scratch_shapes=[
            pltpu.VMEM((2, HALF, 2048), BF),
            pltpu.VMEM((768, 2048), BF),
            pltpu.VMEM((2, HALF, 768), F32),
            pltpu.VMEM((2, HALF, 256), BF),
            pltpu.VMEM((2, 128, 128), F32),
            pltpu.SemaphoreType.DMA((32,)),
        ],
        compiler_params=pltpu.CompilerParams(vmem_limit_bytes=VMEM_LIMIT),
        name="mix",
    )(idx, *xo, *xp, *w, bias, gain, mat, dst)


def spread(out_s, x, p0, p1, p2, p3):
    for z in range(2):
        p0[z] = out_s[z * 4 + x]
        for k, ref in ((1, p1), (2, p2), (3, p3)):
            ref[z] = out_s[z * 4 + ((x + k) & 3)].astype(BF)


PARTS = (
    jax.ShapeDtypeStruct((2, HALF, 256), F32),
    jax.ShapeDtypeStruct((2, HALF, 256), BF),
    jax.ShapeDtypeStruct((2, HALF, 256), BF),
    jax.ShapeDtypeStruct((2, HALF, 256), BF),
)


def out_kernel(
    idx, a_ref, b_ref, u0, u1, u2, u3, u4, v0, v1, v2, v3, v4,
    p0, p1, p2, p3, ocat, wcat, out_s, sems,
):
    copies = [(a_ref, ocat.at[:, 0:256]), (b_ref, ocat.at[:, 256:512])]
    for cc, refs in ((0, (u0, u1, u2, u3, u4)), (1, (v0, v1, v2, v3, v4))):
        for ref, j, r in weight_blocks(refs, idx):
            at = cc * 256 + j * 128
            copies.append((ref, wcat.at[r, at : at + 128, :]))
    for cp in copy_all(copies, sems):
        cp.wait()

    def block(r, unused):
        out_s[r] = dot_nn(ocat[...], wcat[r])
        return unused

    lax.fori_loop(0, 8, block, 0)
    spread(out_s, idx[3], p0, p1, p2, p3)


def out_call(idx, a, b, u, v):
    return pl.pallas_call(
        out_kernel,
        out_shape=PARTS,
        in_specs=[sspec()] + [anyspec()] * 12,
        out_specs=(vspec(),) * 4,
        scratch_shapes=[
            pltpu.VMEM((HALF, 512), BF),
            pltpu.VMEM((8, 512, 256), BF),
            pltpu.VMEM((8, HALF, 256), F32),
            pltpu.SemaphoreType.DMA((34,)),
        ],
        compiler_params=pltpu.CompilerParams(vmem_limit_bytes=VMEM_LIMIT),
        name="outp",
    )(idx, a, b, *u, *v)


def mlp_kernel(
    idx, x0, x1, x2, x3, x4, g0, g1, g2, g3, g4, h0, h1, h2, h3, h4,
    d0, d1, d2, d3, d4, e0, e1, e2, e3, e4, gain_ref,
    p0, p1, p2, p3, xcat, wg, wd, hid, out_s, sems,
):
    x = idx[3]
    first = copy_all(x_copies((x0, x1, x2, x3, x4), xcat, x), sems)
    copies = []
    for cc, refs in ((0, (g0, g1, g2, g3, g4)), (1, (h0, h1, h2, h3, h4))):
        for ref, j, r in weight_blocks(refs, idx):
            at = cc * 704 + j * 352
            copies.append((ref, wg.at[:, at : at + 352, col(r)]))
    second = copy_all(copies, sems.at[8:40])
    copies = []
    for cc, refs in ((0, (d0, d1, d2, d3, d4)), (1, (e0, e1, e2, e3, e4))):
        for ref, j, r in weight_blocks(refs, idx):
            at = cc * 704 + j * 352
            copies.append((ref, wd.at[at : at + 352, col(r)]))
    third = copy_all(copies, sems.at[40:72])
    for cp in first:
        cp.wait()

    def normalize(i, unused):
        rows = pl.ds(pl.multiple_of(i * 48, 16), 48)
        r = xcat[rows, :].astype(F32)
        ms = jnp.mean(r * r, axis=-1, keepdims=True)
        xcat[rows, :] = (r * lax.rsqrt(ms + EPS) * gain_ref[...]).astype(BF)
        return unused

    lax.fori_loop(0, 11, normalize, 0)
    for cp in second:
        cp.wait()

    def expand(i, unused):
        rows = pl.ds(pl.multiple_of(i * 176, 16), 176)
        xv = xcat[rows, :]
        gate = dot_nt(xv, wg[0])
        up = dot_nt(xv, wg[1])
        hid[rows, :] = (gate / (1.0 + jnp.exp(-gate)) * up).astype(BF)
        return unused

    lax.fori_loop(0, 3, expand, 0)
    for cp in third:
        cp.wait()

    def block(r, unused):
        out_s[r] = dot_nn(hid[...], wd[:, col(r)])
        return unused

    lax.fori_loop(0, 8, block, 0)
    spread(out_s, x, p0, p1, p2, p3)


def mlp_call(idx, xs, g, h, d, e, gain):
    return pl.pallas_call(
        mlp_kernel,
        out_shape=PARTS,
        in_specs=[sspec()] + [anyspec()] * 25 + [vspec()],
        out_specs=(vspec(),) * 4,
        scratch_shapes=[
            pltpu.VMEM((HALF, 2048), BF),
            pltpu.VMEM((2, 1408, 2048), BF),
            pltpu.VMEM((1408, 2048), BF),
            pltpu.VMEM((HALF, 1408), BF),
            pltpu.VMEM((8, HALF, 256), F32),
            pltpu.SemaphoreType.DMA((72,)),
        ],
        compiler_params=pltpu.CompilerParams(vmem_limit_bytes=VMEM_LIMIT),
        name="mlp",
    )(idx, *xs, *g, *h, *d, *e, gain)


def swap(value, axis):
    return shift(value, axis, 1)


def z_gather(local):
    perm = lambda step: [(i, (i + step) % 4) for i in range(4)]
    return jnp.stack([local] + [lax.ppermute(local, ("zh", "zl"), perm(-k)) for k in (1, 2, 3)])


def after(value, *others):
    return lax.optimization_barrier((value,) + others)[0]


def reduce_parts(parts):
    p0, p1, p2, p3 = parts
    r2 = shift(p2, "x", 2)
    r1 = shift(p1, "x", 1)
    r3 = shift(p3, "x", -1)
    return p0 + r1.astype(F32) + r2.astype(F32) + r3.astype(F32)


def on_device(
    prompt_tokens, decode_tokens, prompt_lengths, decode_states, w_fio, forget_bias,
    head_gain, w_out, mlp_gain, w_gu, w_down,
):
    ax = {name: lax.axis_index(name) for name in SIZES}
    zl = ax["zl"]
    length = jnp.where(zl == 0, prompt_lengths[0], prompt_lengths[1])
    idx = jnp.stack([ax["y"], ax["zh"], zl, ax["x"], ax["c"], length]).astype(jnp.int32)

    rows = jnp.concatenate(
        [
            prompt_tokens.reshape(2, 2, 512, 128),
            decode_tokens.reshape(2, 2, 1, 128),
            jnp.zeros((2, 2, HALF - 513, 128), BF),
        ],
        axis=2,
    ).reshape(4, HALF, 128)
    got = lax.all_to_all(rows, ("zl", "c"), 0, 0, tiled=True)
    x_own = got.reshape(2, 2, HALF, 128).transpose(0, 2, 1, 3).reshape(2, HALF, 256)

    fio = z_gather(w_fio.astype(BF).T)
    fio = ring_gather(fio, "y")
    xs = ring_gather(x_own, "x")
    xp = [swap(v, "c") for v in xs]

    wo = z_gather(after(w_out, x_own, fio[0]).astype(BF))
    wo = ring_gather(after(wo, fio[1], fio[4]), "y")
    wo2 = [swap(v, "c") for v in wo]
    gu = z_gather(after(w_gu, wo[0]).astype(BF).T.reshape(2, 352, 256))
    gu = ring_gather(after(gu, fio[2], fio[3], wo[1], wo[4]), "y")
    gu2 = [swap(v, "c") for v in gu]
    wd = z_gather(after(w_down, gu[0]).astype(BF))
    wd = ring_gather(after(wd, gu[2], gu[3]), "y")
    wd2 = [swap(v, "c") for v in wd]

    small = jnp.stack([forget_bias, head_gain])
    small2 = swap(small, "zl")
    bias = jnp.stack([small[0], small2[0]])
    gain = jnp.stack([small[1], small2[1]])
    ds = decode_states.reshape(2, 2, 128, 128)
    ds_keep = jnp.where(zl == 0, ds[0], ds[1])
    ds_send = jnp.where(zl == 0, ds[1], ds[0])
    dst = jnp.stack([ds_keep, swap(ds_send, "zl")])

    ho, hs, states = mix_call(idx, xs, xp, fio, bias, gain, dst)
    hr = swap(hs, "c")
    mine, other = states[0], swap(states[1], "zl")
    decode_next = jnp.where(
        zl == 0,
        jnp.concatenate([mine[:2], other[:2]]),
        jnp.concatenate([other[:2], mine[:2]]),
    ).reshape(4, 1, 128, 128)
    prompt_states = jnp.where(
        zl == 0, jnp.stack([mine[2], other[2]]), jnp.stack([other[2], mine[2]])
    ).reshape(2, 1, 128, 128)

    attention = reduce_parts(out_call(idx, ho, hr, wo, wo2))
    attention = after(attention, decode_next, prompt_states)
    residual = (x_own.astype(F32) + attention).astype(BF)
    rs = ring_gather(residual, "x")
    down = reduce_parts(mlp_call(idx, rs, gu, gu2, wd, wd2, mlp_gain.reshape(1, 2048)))
    layer = (residual.astype(F32) + down).astype(BF)
    layer = layer.reshape(2, HALF, 2, 128).transpose(0, 2, 1, 3).reshape(4, HALF, 128)
    back = lax.all_to_all(layer, ("zl", "c"), 0, 0, tiled=True)
    prompt_out = back[:, :512].reshape(2, 1024, 128)
    decode_out = back[:, 512]
    return (prompt_out, decode_out, prompt_states, decode_next)


def solution(mesh):
    wide = Mesh(mesh.devices.reshape(tuple(SIZES.values())), tuple(SIZES))
    req = ("y", "zh")
    mlp = ("zl", "x", "c")
    return jax.shard_map(
        on_device,
        mesh=wide,
        in_specs=(
            P(req, None, mlp),
            P(req, mlp),
            P(req),
            P(req, mlp, None, None),
            P(req, mlp),
            P(mlp),
            P(mlp),
            P(mlp, req),
            P(),
            P(req, mlp),
            P(mlp, req),
        ),
        out_specs=(
            P(req, None, mlp),
            P(req, mlp),
            P(req, mlp, None, None),
            P(req, mlp, None, None),
        ),
        check_vma=False,
    )
```

```python
import functools

import jax
import jax.numpy as jnp
import numpy as np
from jax import lax
from jax.experimental import pallas as pl
from jax.experimental.layout import Layout, with_layout_constraint
from jax.experimental.pallas import tpu as pltpu
from jax.sharding import Mesh, PartitionSpec as P

EPS = 1e-5
HALF = 528
CH = 128
LEVELS = 7
BF = jnp.bfloat16
F32 = jnp.float32
SIZES = {"y": 4, "zh": 2, "zl": 2, "x": 4, "c": 2}
VMEM_LIMIT = 60 * 1024 * 1024


def shift(value, axis, step):
    n = SIZES[axis]
    return lax.ppermute(value, axis, [(i, (i + step) % n) for i in range(n)])


def ring_gather(own, axis):
    n = own.shape[0] // 2
    before = shift(own, axis, 1)
    ahead = shift(own, axis, -1)
    far0 = shift(before[:n], axis, 1)
    far1 = shift(ahead[n:], axis, -1)
    return [own, ahead, far0, far1, before]


def piece(refs, step, part):
    if step == 2:
        return refs[2 + part].at[0]
    return refs[{0: 0, 1: 1, 3: 4}[step]].at[part]


def level_matrix():
    t = np.arange(CH)[:, None]
    u = np.arange(CH)[None, :]
    rows = []
    for level in range(LEVELS):
        b = 1 << level
        ref = (t // (2 * b)) * 2 * b + b - 1
        late = (t % (2 * b)) >= b
        rows.append(np.where(late, (u > ref) & (u <= t), (u > t) & (u <= ref)))
    rows.append(u <= t)
    rows.append(u > t)
    return np.concatenate(rows, 0).astype(np.float32)


def dot_nt(a, b):
    return lax.dot_general(a, b, (((1,), (1,)), ((), ())), preferred_element_type=F32)


def dot_tn(a, b):
    return lax.dot_general(a, b, (((0,), (0,)), ((), ())), preferred_element_type=F32)


def dot_nn(a, b):
    return jnp.dot(a, b, preferred_element_type=F32)


def copy_all(copies, sems):
    started = []
    for i, (src, dst) in enumerate(copies):
        cp = pltpu.make_async_copy(src, dst, sems.at[i])
        cp.start()
        started.append(cp)
    return started


def col(r):
    return pl.ds(pl.multiple_of(r * 256, 256), 256)


def x_copies(refs, cat, x):
    out = []
    for k in range(4):
        for z in range(2):
            r = z * 4 + ((x + k) & 3)
            out.append((piece(refs, k, z), cat.at[:, col(r)]))
    return out


def head_out(o, gain):
    ms = jnp.mean(o * o, axis=-1, keepdims=True)
    return o * lax.rsqrt(ms + EPS) * gain


def mix_kernel(
    idx, xo0, xo1, xo2, xo3, xo4, xpm, xp2, xp3, w_ref,
    bias_ref, gain_ref, mat_ref, dst_ref,
    own_ref, other_ref, keep_ref, send_ref,
    xcat, wcat, mix, oscr, carry, sems,
):
    x, c, length = idx[3], idx[4], idx[5]
    copies = x_copies((xo0, xo1, xo2, xo3, xo4), xcat.at[0:HALF], x)
    copies += x_copies((xpm.at[0], xpm.at[1], xp2, xp3, xpm.at[2]), xcat.at[HALF : 2 * HALF], x)
    for i in range(16):
        at = pl.multiple_of(((i & 1) ^ idx[2]) * 384, 128)
        r = i // 2
        copies.append((w_ref.at[i, 0:384], wcat.at[pl.ds(at, 384), r * 256 : (r + 1) * 256]))
    for cp in copy_all(copies, sems):
        cp.wait()

    def project(i, unused):
        part = dot_nt(xcat[...], wcat[pl.ds(pl.multiple_of(i * 256, 256), 256), :])
        mix[c, :, col(i)] = part[:HALF]
        mix[1 - c, :, col(i)] = part[HALF:]
        return unused

    lax.fori_loop(0, 3, project, 0)
    carry[...] = jnp.zeros_like(carry)
    t = lax.broadcasted_iota(jnp.int32, (CH, CH), 0)
    s = lax.broadcasted_iota(jnp.int32, (CH, CH), 1)
    pair = jnp.where(t > s, t ^ s, 0)
    diag = t == s
    row = lax.broadcasted_iota(jnp.int32, (CH, 128), 0)

    def chunk(n, unused):
        h = n // 4
        rows = pl.ds(pl.multiple_of((n % 4) * CH, CH), CH)
        alive = (row + n * CH) < length
        for j in range(2):
            z = mix[h, rows, j * 384 : j * 384 + 128] + bias_ref[j : j + 1, :]
            v = mix[h, rows, j * 384 + 128 : j * 384 + 256].astype(BF)
            q = mix[h, rows, j * 384 + 256 : j * 384 + 384]
            e = jnp.exp(-jnp.abs(z))
            logf = jnp.where(alive, jnp.minimum(z, 0.0) - jnp.log1p(e), 0.0)
            inv = 1.0 / (1.0 + e)
            k = jnp.where(alive, jnp.where(z >= 0, e * inv, inv), 0.0)
            hi = logf.astype(BF)
            lo = (logf - hi.astype(F32)).astype(BF)
            d = dot_nn(mat_ref[...], jnp.concatenate([hi, lo], axis=1))
            decay = jnp.exp(d[:, :128] + d[:, 128:])
            scores = jnp.where(diag, dot_nt(q.astype(BF), k.astype(BF)), 0.0)
            for level in range(LEVELS):
                el = decay[level * CH : (level + 1) * CH]
                part = dot_nt((q * el).astype(BF), (k * el).astype(BF))
                scores = jnp.where((pair >> level) == 1, part, scores)
            es = decay[LEVELS * CH : (LEVELS + 1) * CH]
            ee = decay[(LEVELS + 1) * CH :]
            held = carry[j]
            o = dot_nn(scores.astype(BF), v) + dot_nt((q * es).astype(BF), held.astype(BF))
            o = jnp.where(alive, o, 0.0)
            carry[j] = held * es[CH - 1 :, :] + dot_tn(v, (k * ee).astype(BF))
            oscr[h, rows, j * 128 : (j + 1) * 128] = head_out(o, gain_ref[j : j + 1, :]).astype(BF)
        return unused

    lax.fori_loop(0, 8, chunk, 0)
    first = lax.broadcasted_iota(jnp.int32, (16, 128), 0) == 0
    for h in range(2):
        for j in range(2):
            z = mix[h, 512:513, j * 384 : j * 384 + 128] + bias_ref[j : j + 1, :]
            v = mix[h, 512:513, j * 384 + 128 : j * 384 + 256]
            q = mix[h, 512:513, j * 384 + 256 : j * 384 + 384]
            e = jnp.exp(-jnp.abs(z))
            inv = 1.0 / (1.0 + e)
            f = jnp.where(z >= 0, inv, e * inv)
            k = jnp.where(z >= 0, e * inv, inv)
            ft = jnp.broadcast_to(f, (128, 128)).T
            kt = jnp.broadcast_to(k, (128, 128)).T
            qt = jnp.broadcast_to(q, (128, 128)).T
            nxt = ft * dst_ref[j, h] + kt * v
            (keep_ref, send_ref)[j][h] = nxt
            o = head_out(jnp.sum(nxt * qt, axis=0, keepdims=True), gain_ref[j : j + 1, :])
            wide = jnp.where(first, jnp.broadcast_to(o, (16, 128)), 0.0)
            oscr[h, 512:528, j * 128 : (j + 1) * 128] = wide.astype(BF)
    for j in range(2):
        (keep_ref, send_ref)[j][2] = carry[j].T
    own_ref[...] = oscr[c]
    other_ref[...] = oscr[1 - c]


def anyspec():
    return pl.BlockSpec(memory_space=pl.ANY)


def vspec():
    return pl.BlockSpec(memory_space=pltpu.VMEM)


def sspec():
    return pl.BlockSpec(memory_space=pltpu.SMEM)


def cost(us):
    return pl.CostEstimate(flops=us, transcendentals=0, bytes_accessed=us)


def mix_call(idx, xo, xp, w, bias, gain, dst):
    mat = jnp.asarray(level_matrix(), BF)
    return pl.pallas_call(
        mix_kernel,
        out_shape=(
            jax.ShapeDtypeStruct((HALF, 256), BF),
            jax.ShapeDtypeStruct((HALF, 256), BF),
            jax.ShapeDtypeStruct((3, 128, 128), F32),
            jax.ShapeDtypeStruct((3, 128, 128), F32),
        ),
        in_specs=[sspec()] + [anyspec()] * 9 + [vspec()] * 4,
        out_specs=(vspec(),) * 4,
        scratch_shapes=[
            pltpu.VMEM((2 * HALF, 2048), BF),
            pltpu.VMEM((768, 2048), BF),
            pltpu.VMEM((2, HALF, 768), F32),
            pltpu.VMEM((2, HALF, 256), BF),
            pltpu.VMEM((2, 128, 128), F32),
            pltpu.SemaphoreType.DMA((32,)),
        ],
        compiler_params=pltpu.CompilerParams(vmem_limit_bytes=VMEM_LIMIT),
        cost_estimate=cost(24),
        name="mix",
    )(idx, *xo, *xp, w, bias, gain, mat, dst)


def spread(out_s, x, p0, p1, p2, p3):
    for z in range(2):
        p0[z] = out_s[z * 4 + x]
        for k, ref in ((1, p1), (2, p2), (3, p3)):
            ref[z] = out_s[z * 4 + ((x + k) & 3)].astype(BF)


PARTS = (
    jax.ShapeDtypeStruct((2, HALF, 256), F32),
    jax.ShapeDtypeStruct((2, HALF, 256), BF),
    jax.ShapeDtypeStruct((2, HALF, 256), BF),
    jax.ShapeDtypeStruct((2, HALF, 256), BF),
)


def out_kernel(
    idx, a_ref, b_ref, u_ref, v_ref,
    p0, p1, p2, p3, ocat, wcat, out_s, sems,
):
    copies = [(a_ref, ocat.at[:, 0:256]), (b_ref, ocat.at[:, 256:512])]
    for i in range(16):
        for cc in range(2):
            src = v_ref.at[i] if cc else u_ref.at[i, 384:512]
            at = pl.multiple_of(cc * 256 + ((i & 1) ^ idx[2]) * 128, 128)
            copies.append((src, wcat.at[i // 2, pl.ds(at, 128), :]))
    for cp in copy_all(copies, sems):
        cp.wait()

    def block(r, unused):
        out_s[r] = dot_nn(ocat[...], wcat[r])
        return unused

    lax.fori_loop(0, 8, block, 0)
    spread(out_s, idx[3], p0, p1, p2, p3)


def out_call(idx, a, b, u, v):
    return pl.pallas_call(
        out_kernel,
        out_shape=PARTS,
        in_specs=[sspec()] + [anyspec()] * 4,
        out_specs=(vspec(),) * 4,
        scratch_shapes=[
            pltpu.VMEM((HALF, 512), BF),
            pltpu.VMEM((8, 512, 256), BF),
            pltpu.VMEM((8, HALF, 256), F32),
            pltpu.SemaphoreType.DMA((34,)),
        ],
        compiler_params=pltpu.CompilerParams(vmem_limit_bytes=VMEM_LIMIT),
        cost_estimate=cost(7),
        name="outp",
    )(idx, a, b, u, v)


def mlp_kernel(
    idx, x0, x1, x2, x3, x4, g_ref, h_ref, gain_ref,
    p0, p1, p2, p3, xcat, wg, wd, hid, out_s, sems,
):
    x = idx[3]
    first = copy_all(x_copies((x0, x1, x2, x3, x4), xcat, x), sems)
    copies = []
    for cc, ref in ((0, g_ref), (1, h_ref)):
        for i in range(16):
            at, r = cc * 704 + (i & 1) * 352, i // 2
            for g in range(2):
                dst = wg.at[g, at : at + 352, r * 256 : (r + 1) * 256]
                copies.append((ref.at[i, g * 352 : (g + 1) * 352], dst))
    second = copy_all(copies, sems.at[8:72])
    copies = []
    for cc, ref in ((0, g_ref), (1, h_ref)):
        for i in range(16):
            at, r = cc * 704 + (i & 1) * 352, i // 2
            dst = wd.at[at : at + 352, r * 256 : (r + 1) * 256]
            copies.append((ref.at[i, 704:1056], dst))
    third = copy_all(copies, sems.at[72:104])
    for cp in first:
        cp.wait()

    def normalize(i, unused):
        rows = pl.ds(pl.multiple_of(i * 48, 16), 48)
        r = xcat[rows, :].astype(F32)
        ms = jnp.mean(r * r, axis=-1, keepdims=True)
        xcat[rows, :] = (r * lax.rsqrt(ms + EPS) * gain_ref[...]).astype(BF)
        return unused

    lax.fori_loop(0, 11, normalize, 0)
    for cp in second:
        cp.wait()

    for lo, hi in ((0, 768), (768, 1408)):
        gate = dot_nt(xcat[...], wg[0, lo:hi, :])
        up = dot_nt(xcat[...], wg[1, lo:hi, :])
        hid[:, lo:hi] = (gate / (1.0 + jnp.exp(-gate)) * up).astype(BF)
    for cp in third:
        cp.wait()

    def block(r, unused):
        out_s[r] = dot_nn(hid[...], wd[:, col(r)])
        return unused

    lax.fori_loop(0, 8, block, 0)
    spread(out_s, x, p0, p1, p2, p3)


def mlp_call(idx, xs, g, h, gain):
    return pl.pallas_call(
        mlp_kernel,
        out_shape=PARTS,
        in_specs=[sspec()] + [anyspec()] * 7 + [vspec()],
        out_specs=(vspec(),) * 4,
        scratch_shapes=[
            pltpu.VMEM((HALF, 2048), BF),
            pltpu.VMEM((2, 1408, 2048), BF),
            pltpu.VMEM((1408, 2048), BF),
            pltpu.VMEM((HALF, 1408), BF),
            pltpu.VMEM((8, HALF, 256), F32),
            pltpu.SemaphoreType.DMA((104,)),
        ],
        compiler_params=pltpu.CompilerParams(vmem_limit_bytes=VMEM_LIMIT),
        cost_estimate=cost(20),
        name="mlp",
    )(idx, *xs, g, h, gain)


def swap(value, axis):
    return shift(value, axis, 1)


def after(value, *others):
    return lax.optimization_barrier((value,) + others)[0]


def reduce_parts(parts, *others):
    p0, p1, p2, p3 = parts
    r2 = shift(p2, "x", 2)
    r1 = shift(p1, "x", 1)
    r3 = shift(p3, "x", -1)
    r1 = after(r1, r2, r3, *others)
    return p0 + r1.astype(F32) + r2.astype(F32) + r3.astype(F32)


def on_device(
    prompt_tokens, decode_tokens, prompt_lengths, decode_states, w_fio, forget_bias,
    head_gain, w_out, mlp_gain, w_gu, w_down,
):
    ax = {name: lax.axis_index(name) for name in SIZES}
    zl = ax["zl"]
    length = jnp.where(zl == 0, prompt_lengths[0], prompt_lengths[1])
    idx = jnp.stack([ax["y"], ax["zh"], zl, ax["x"], ax["c"], length]).astype(jnp.int32)

    rows = jnp.concatenate(
        [
            prompt_tokens.reshape(2, 2, 512, 128),
            decode_tokens.reshape(2, 2, 1, 128),
            jnp.zeros((2, 2, HALF - 513, 128), BF),
        ],
        axis=2,
    ).reshape(4, HALF, 128)
    got = lax.all_to_all(rows, ("zl", "c"), 0, 0, tiled=True)
    x_own = got.reshape(2, 2, HALF, 128).transpose(0, 2, 1, 3).reshape(2, HALF, 256)

    small = jnp.stack([forget_bias, head_gain])
    ds = decode_states.reshape(2, 256, 128)
    ds_keep = jnp.where(zl == 0, ds[0], ds[1])
    ds_send = jnp.where(zl == 0, ds[1], ds[0])
    other = swap(jnp.concatenate([ds_send, small]), "zl")
    early = jnp.concatenate([w_fio.astype(BF).T, w_out.astype(BF)])
    early = with_layout_constraint(early, Layout((0, 1)))
    early = lax.all_gather(early, ("y", "zh", "zl")).reshape(16, 512, 256)
    x_own, other = lax.optimization_barrier((x_own, other))
    bias = jnp.stack([small[0], other[256]])
    gain = jnp.stack([small[1], other[257]])
    dst = jnp.stack([ds_keep, other[:256]]).reshape(2, 2, 128, 128)

    x_before, x_ahead = shift(x_own, "x", 1), shift(x_own, "x", -1)
    x_mid = swap(jnp.stack([x_own, x_ahead, x_before]), "c")
    xs = [x_own, x_ahead, shift(x_before[:1], "x", 1), shift(x_ahead[1:], "x", -1), x_before]
    xp = [x_mid, swap(xs[2], "c"), swap(xs[3], "c")]
    wo2 = swap(early[:, 384:], "c")
    late = jnp.concatenate([w_gu.astype(BF).T, w_down.astype(BF)])
    late = after(late, early, *xp)
    late = lax.all_gather(late, ("y", "zh", "zl")).reshape(16, 1056, 256)

    ho, hs, mine, sent = mix_call(idx, xs, xp, early, bias, gain, dst)
    hr = swap(hs, "c")
    other = swap(sent, "zl")
    decode_next = jnp.where(
        zl == 0,
        jnp.concatenate([mine[:2], other[:2]]),
        jnp.concatenate([other[:2], mine[:2]]),
    ).reshape(4, 1, 128, 128)
    prompt_states = jnp.where(
        zl == 0, jnp.stack([mine[2], other[2]]), jnp.stack([other[2], mine[2]])
    ).reshape(2, 1, 128, 128)

    attention = reduce_parts(out_call(idx, ho, hr, early, wo2), other)
    residual = (x_own.astype(F32) + attention).astype(BF)
    rs = ring_gather(residual, "x")
    late2 = swap(after(late, rs[1], rs[4]), "c")
    down = reduce_parts(mlp_call(idx, rs, late, late2, mlp_gain.reshape(1, 2048)))
    layer = (residual.astype(F32) + down).astype(BF)
    layer = layer.reshape(2, HALF, 2, 128).transpose(0, 2, 1, 3).reshape(4, HALF, 128)
    back = lax.all_to_all(layer, ("zl", "c"), 0, 0, tiled=True)
    prompt_out = back[:, :512].reshape(2, 1024, 128)
    decode_out = back[:, 512]
    return (prompt_out, decode_out, prompt_states, decode_next)


def solution(mesh):
    wide = Mesh(mesh.devices.reshape(tuple(SIZES.values())), tuple(SIZES))
    req = ("y", "zh")
    mlp = ("zl", "x", "c")
    return jax.shard_map(
        on_device,
        mesh=wide,
        in_specs=(
            P(req, None, mlp),
            P(req, mlp),
            P(req),
            P(req, mlp, None, None),
            P(req, mlp),
            P(mlp),
            P(mlp),
            P(mlp, req),
            P(),
            P(req, mlp),
            P(mlp, req),
        ),
        out_specs=(
            P(req, None, mlp),
            P(req, mlp),
            P(req, mlp, None, None),
            P(req, mlp, None, None),
        ),
        check_vma=False,
    )
```

```python
import functools

import jax
import jax.numpy as jnp
import numpy as np
from jax import lax
from jax.experimental import pallas as pl
from jax.experimental.layout import Layout, with_layout_constraint
from jax.experimental.pallas import tpu as pltpu
from jax.sharding import Mesh, PartitionSpec as P

EPS = 1e-5
HALF = 528
CH = 128
LEVELS = 7
BF = jnp.bfloat16
F32 = jnp.float32
SIZES = {"y": 4, "zh": 2, "zl": 2, "x": 4, "c": 2}
VMEM_LIMIT = 60 * 1024 * 1024


def shift(value, axis, step):
    n = SIZES[axis]
    return lax.ppermute(value, axis, [(i, (i + step) % n) for i in range(n)])


def ring_gather(own, axis):
    n = own.shape[0] // 2
    before = shift(own, axis, 1)
    ahead = shift(own, axis, -1)
    far0 = shift(before[:n], axis, 1)
    far1 = shift(ahead[n:], axis, -1)
    return [own, ahead, far0, far1, before]


def piece(refs, step, part):
    if step == 2:
        return refs[2 + part].at[0]
    return refs[{0: 0, 1: 1, 3: 4}[step]].at[part]


def level_matrix():
    t = np.arange(CH)[:, None]
    u = np.arange(CH)[None, :]
    rows = []
    for level in range(LEVELS):
        b = 1 << level
        ref = (t // (2 * b)) * 2 * b + b - 1
        late = (t % (2 * b)) >= b
        rows.append(np.where(late, (u > ref) & (u <= t), (u > t) & (u <= ref)))
    rows.append(u <= t)
    rows.append(u > t)
    return np.concatenate(rows, 0).astype(np.float32)


def dot_nt(a, b):
    return lax.dot_general(a, b, (((1,), (1,)), ((), ())), preferred_element_type=F32)


def dot_tn(a, b):
    return lax.dot_general(a, b, (((0,), (0,)), ((), ())), preferred_element_type=F32)


def dot_nn(a, b):
    return jnp.dot(a, b, preferred_element_type=F32)


def copy_all(copies, sems):
    started = []
    for i, (src, dst) in enumerate(copies):
        cp = pltpu.make_async_copy(src, dst, sems.at[i])
        cp.start()
        started.append(cp)
    return started


def col(r):
    return pl.ds(pl.multiple_of(r * 256, 256), 256)


def x_copies(refs, cat, x):
    out = []
    for k in range(4):
        for z in range(2):
            r = z * 4 + ((x + k) & 3)
            out.append((piece(refs, k, z), cat.at[:, col(r)]))
    return out


def head_out(o, gain):
    ms = jnp.mean(o * o, axis=-1, keepdims=True)
    return o * lax.rsqrt(ms + EPS) * gain


def mix_kernel(
    idx, xo0, xo1, xo2, xo3, xo4, xpm, xp2, xp3, w_ref,
    bias_ref, gain_ref, mat_ref, dst_ref,
    own_ref, other_ref, keep_ref, send_ref,
    xcat, wcat, mix, oscr, carry, sems,
):
    x, c, length = idx[3], idx[4], idx[5]
    copies = x_copies((xo0, xo1, xo2, xo3, xo4), xcat.at[0:HALF], x)
    copies += x_copies((xpm.at[0], xpm.at[1], xp2, xp3, xpm.at[2]), xcat.at[HALF : 2 * HALF], x)
    for i in range(16):
        at = pl.multiple_of(((i & 1) ^ idx[2]) * 384, 128)
        r = i // 2
        copies.append((w_ref.at[i, 0:384], wcat.at[pl.ds(at, 384), r * 256 : (r + 1) * 256]))
    for cp in copy_all(copies, sems):
        cp.wait()

    def project(i, unused):
        part = dot_nt(xcat[...], wcat[pl.ds(pl.multiple_of(i * 256, 256), 256), :])
        mix[c, :, col(i)] = part[:HALF]
        mix[1 - c, :, col(i)] = part[HALF:]
        return unused

    lax.fori_loop(0, 3, project, 0)
    carry[...] = jnp.zeros_like(carry)
    t = lax.broadcasted_iota(jnp.int32, (CH, CH), 0)
    s = lax.broadcasted_iota(jnp.int32, (CH, CH), 1)
    pair = jnp.where(t > s, t ^ s, 0)
    diag = t == s
    row = lax.broadcasted_iota(jnp.int32, (CH, 128), 0)

    def chunk(n, unused):
        h = n // 4
        rows = pl.ds(pl.multiple_of((n % 4) * CH, CH), CH)
        alive = (row + n * CH) < length
        for j in range(2):
            z = mix[h, rows, j * 384 : j * 384 + 128] + bias_ref[j : j + 1, :]
            v = mix[h, rows, j * 384 + 128 : j * 384 + 256].astype(BF)
            q = mix[h, rows, j * 384 + 256 : j * 384 + 384]
            e = jnp.exp(-jnp.abs(z))
            logf = jnp.where(alive, jnp.minimum(z, 0.0) - jnp.log1p(e), 0.0)
            inv = 1.0 / (1.0 + e)
            k = jnp.where(alive, jnp.where(z >= 0, e * inv, inv), 0.0)
            hi = logf.astype(BF)
            lo = (logf - hi.astype(F32)).astype(BF)
            d = dot_nn(mat_ref[...], jnp.concatenate([hi, lo], axis=1))
            decay = jnp.exp(d[:, :128] + d[:, 128:])
            scores = jnp.where(diag, dot_nt(q.astype(BF), k.astype(BF)), 0.0)
            for level in range(LEVELS):
                el = decay[level * CH : (level + 1) * CH]
                part = dot_nt((q * el).astype(BF), (k * el).astype(BF))
                scores = jnp.where((pair >> level) == 1, part, scores)
            es = decay[LEVELS * CH : (LEVELS + 1) * CH]
            ee = decay[(LEVELS + 1) * CH :]
            held = carry[j]
            o = dot_nn(scores.astype(BF), v) + dot_nt((q * es).astype(BF), held.astype(BF))
            o = jnp.where(alive, o, 0.0)
            carry[j] = held * es[CH - 1 :, :] + dot_tn(v, (k * ee).astype(BF))
            oscr[h, rows, j * 128 : (j + 1) * 128] = head_out(o, gain_ref[j : j + 1, :]).astype(BF)
        return unused

    lax.fori_loop(0, 8, chunk, 0, unroll=2)
    first = lax.broadcasted_iota(jnp.int32, (16, 128), 0) == 0
    for h in range(2):
        for j in range(2):
            z = mix[h, 512:513, j * 384 : j * 384 + 128] + bias_ref[j : j + 1, :]
            v = mix[h, 512:513, j * 384 + 128 : j * 384 + 256]
            q = mix[h, 512:513, j * 384 + 256 : j * 384 + 384]
            e = jnp.exp(-jnp.abs(z))
            inv = 1.0 / (1.0 + e)
            f = jnp.where(z >= 0, inv, e * inv)
            k = jnp.where(z >= 0, e * inv, inv)
            ft = jnp.broadcast_to(f, (128, 128)).T
            kt = jnp.broadcast_to(k, (128, 128)).T
            qt = jnp.broadcast_to(q, (128, 128)).T
            nxt = ft * dst_ref[j, h] + kt * v
            (keep_ref, send_ref)[j][h] = nxt
            o = head_out(jnp.sum(nxt * qt, axis=0, keepdims=True), gain_ref[j : j + 1, :])
            wide = jnp.where(first, jnp.broadcast_to(o, (16, 128)), 0.0)
            oscr[h, 512:528, j * 128 : (j + 1) * 128] = wide.astype(BF)
    for j in range(2):
        (keep_ref, send_ref)[j][2] = carry[j].T
    own_ref[...] = oscr[c]
    other_ref[...] = oscr[1 - c]


def anyspec():
    return pl.BlockSpec(memory_space=pl.ANY)


def vspec():
    return pl.BlockSpec(memory_space=pltpu.VMEM)


def sspec():
    return pl.BlockSpec(memory_space=pltpu.SMEM)


def cost(us):
    return pl.CostEstimate(flops=us, transcendentals=0, bytes_accessed=us)


def mix_call(idx, xo, xp, w, bias, gain, dst):
    mat = jnp.asarray(level_matrix(), BF)
    return pl.pallas_call(
        mix_kernel,
        out_shape=(
            jax.ShapeDtypeStruct((HALF, 256), BF),
            jax.ShapeDtypeStruct((HALF, 256), BF),
            jax.ShapeDtypeStruct((3, 128, 128), F32),
            jax.ShapeDtypeStruct((3, 128, 128), F32),
        ),
        in_specs=[sspec()] + [anyspec()] * 9 + [vspec()] * 4,
        out_specs=(vspec(),) * 4,
        scratch_shapes=[
            pltpu.VMEM((2 * HALF, 2048), BF),
            pltpu.VMEM((768, 2048), BF),
            pltpu.VMEM((2, HALF, 768), F32),
            pltpu.VMEM((2, HALF, 256), BF),
            pltpu.VMEM((2, 128, 128), F32),
            pltpu.SemaphoreType.DMA((32,)),
        ],
        compiler_params=pltpu.CompilerParams(vmem_limit_bytes=VMEM_LIMIT),
        cost_estimate=cost(24),
        name="mix",
    )(idx, *xo, *xp, w, bias, gain, mat, dst)


PART = jax.ShapeDtypeStruct((2, HALF, 256), F32)
FAR = jax.ShapeDtypeStruct((1, HALF, 256), BF)


def shapes_of(steps):
    return (FAR, FAR) if steps == (2,) else (PART,) * len(steps)


def put(steps, outs, s, z, value):
    if steps == (2,):
        outs[z][0] = value.astype(BF)
    else:
        outs[s][z] = value


def blocks_of(steps, x):
    for s, k in enumerate(steps):
        for z in range(2):
            yield s * 2 + z, s, z, z * 4 + ((x + k) & 3)


def out_kernel(steps, idx, a_ref, b_ref, u_ref, v_ref, *rest):
    outs, (ocat, wcat, sems) = rest[:-3], rest[-3:]
    copies = [(a_ref, ocat.at[:, 0:256]), (b_ref, ocat.at[:, 256:512])]
    for slot, s, z, r in blocks_of(steps, idx[3]):
        for j in range(2):
            for cc in range(2):
                src = v_ref.at[2 * r + j] if cc else u_ref.at[2 * r + j, 384:512]
                at = pl.multiple_of(cc * 256 + (j ^ idx[2]) * 128, 128)
                copies.append((src, wcat.at[slot, pl.ds(at, 128), :]))
    for cp in copy_all(copies, sems):
        cp.wait()
    for slot, s, z, r in blocks_of(steps, idx[3]):
        put(steps, outs, s, z, dot_nn(ocat[...], wcat[slot]))


def out_call(steps, idx, a, b, u, v):
    n = len(steps)
    return pl.pallas_call(
        functools.partial(out_kernel, steps),
        out_shape=shapes_of(steps),
        in_specs=[sspec()] + [anyspec()] * 4,
        out_specs=(vspec(),) * len(shapes_of(steps)),
        scratch_shapes=[
            pltpu.VMEM((HALF, 512), BF),
            pltpu.VMEM((2 * n, 512, 256), BF),
            pltpu.SemaphoreType.DMA((2 + 8 * n,)),
        ],
        compiler_params=pltpu.CompilerParams(vmem_limit_bytes=VMEM_LIMIT),
        cost_estimate=cost(2 * n),
        name="outp",
    )(idx, a, b, u, v)


def down_copies(steps, x, refs, wd):
    out = []
    for slot, s, z, r in blocks_of(steps, x):
        for j in range(2):
            for cc, ref in enumerate(refs):
                at = cc * 704 + j * 352
                out.append((ref.at[2 * r + j, 704:1056], wd.at[slot, at : at + 352, :]))
    return out


def down_dots(steps, x, hid, wd, outs):
    for slot, s, z, r in blocks_of(steps, x):
        total = dot_nn(hid[0], wd[slot, 0:704, :]) + dot_nn(hid[1], wd[slot, 704:1408, :])
        put(steps, outs, s, z, total)


def mlp_kernel(idx, x0, x1, x2, x3, x4, g_ref, h_ref, gain_ref, hid, q0, q1, xcat, wg, wd, sems):
    x = idx[3]
    started = [copy_all(x_copies((x0, x1, x2, x3, x4), xcat, x), sems)]
    for cc, ref in ((0, g_ref), (1, h_ref)):
        copies = []
        for i in range(16):
            for g in range(2):
                at, r = (i & 1) * 352, i // 2
                dst = wg.at[cc, g, at : at + 352, r * 256 : (r + 1) * 256]
                copies.append((ref.at[i, g * 352 : (g + 1) * 352], dst))
        started.append(copy_all(copies, sems.at[8 + cc * 32 : 40 + cc * 32]))
    last = copy_all(down_copies((2,), x, (g_ref, h_ref), wd), sems.at[72:80])
    for cp in started[0]:
        cp.wait()

    def normalize(i, unused):
        rows = pl.ds(pl.multiple_of(i * 48, 16), 48)
        r = xcat[rows, :].astype(F32)
        ms = jnp.mean(r * r, axis=-1, keepdims=True)
        xcat[rows, :] = (r * lax.rsqrt(ms + EPS) * gain_ref[...]).astype(BF)
        return unused

    lax.fori_loop(0, 11, normalize, 0)
    for cc in range(2):
        for cp in started[1 + cc]:
            cp.wait()
        gate = dot_nt(xcat[...], wg[cc, 0])
        up = dot_nt(xcat[...], wg[cc, 1])
        hid[cc] = (gate / (1.0 + jnp.exp(-gate)) * up).astype(BF)
    for cp in last:
        cp.wait()
    down_dots((2,), x, hid, wd, (q0, q1))


def mlp_call(idx, xs, g, h, gain):
    return pl.pallas_call(
        mlp_kernel,
        out_shape=(jax.ShapeDtypeStruct((2, HALF, 704), BF), FAR, FAR),
        in_specs=[sspec()] + [anyspec()] * 7 + [vspec()],
        out_specs=(vspec(),) * 3,
        scratch_shapes=[
            pltpu.VMEM((HALF, 2048), BF),
            pltpu.VMEM((2, 2, 704, 2048), BF),
            pltpu.VMEM((2, 1408, 256), BF),
            pltpu.SemaphoreType.DMA((80,)),
        ],
        compiler_params=pltpu.CompilerParams(vmem_limit_bytes=VMEM_LIMIT),
        cost_estimate=cost(16),
        name="mlp",
    )(idx, *xs, g, h, gain)


def down_kernel(steps, idx, hid, g_ref, h_ref, p0, p1, p2, wd, sems):
    for cp in copy_all(down_copies(steps, idx[3], (g_ref, h_ref), wd), sems):
        cp.wait()
    down_dots(steps, idx[3], hid, wd, (p0, p1, p2))


def down_call(steps, idx, hid, g, h):
    n = len(steps)
    return pl.pallas_call(
        functools.partial(down_kernel, steps),
        out_shape=shapes_of(steps),
        in_specs=[sspec(), vspec()] + [anyspec()] * 2,
        out_specs=(vspec(),) * n,
        scratch_shapes=[
            pltpu.VMEM((2 * n, 1408, 256), BF),
            pltpu.SemaphoreType.DMA((8 * n,)),
        ],
        compiler_params=pltpu.CompilerParams(vmem_limit_bytes=VMEM_LIMIT),
        cost_estimate=cost(5),
        name="down",
    )(idx, hid, g, h)


def swap(value, axis):
    return shift(value, axis, 1)


def after(value, *others):
    return lax.optimization_barrier((value,) + others)[0]


def reduce_parts(far, rest, *others):
    p1, p3, p0 = rest
    a, b = shift(far[0], "x", 1), shift(far[1], "x", -1)
    a, b = lax.optimization_barrier((a, b))
    keep = (0, 0, 0)
    p1 = (p1 + lax.pad(a.astype(F32), F32(0), ((0, 1, 0), keep, keep))).astype(BF)
    p3 = (p3 + lax.pad(b.astype(F32), F32(0), ((1, 0, 0), keep, keep))).astype(BF)
    r1 = shift(p1, "x", 1)
    r3 = shift(p3, "x", -1)
    r1 = after(r1, r3, *others)
    return p0 + r1.astype(F32) + r3.astype(F32)


def on_device(
    prompt_tokens, decode_tokens, prompt_lengths, decode_states, w_fio, forget_bias,
    head_gain, w_out, mlp_gain, w_gu, w_down,
):
    ax = {name: lax.axis_index(name) for name in SIZES}
    zl = ax["zl"]
    length = jnp.where(zl == 0, prompt_lengths[0], prompt_lengths[1])
    idx = jnp.stack([ax["y"], ax["zh"], zl, ax["x"], ax["c"], length]).astype(jnp.int32)

    rows = jnp.concatenate(
        [
            prompt_tokens.reshape(2, 2, 512, 128),
            decode_tokens.reshape(2, 2, 1, 128),
            jnp.zeros((2, 2, HALF - 513, 128), BF),
        ],
        axis=2,
    ).reshape(4, HALF, 128)
    got = lax.all_to_all(rows, ("zl", "c"), 0, 0, tiled=True)
    x_own = got.reshape(2, 2, HALF, 128).transpose(0, 2, 1, 3).reshape(2, HALF, 256)

    small = jnp.stack([forget_bias, head_gain])
    ds = decode_states.reshape(2, 256, 128)
    ds_keep = jnp.where(zl == 0, ds[0], ds[1])
    ds_send = jnp.where(zl == 0, ds[1], ds[0])
    other = swap(jnp.concatenate([ds_send, small]), "zl")
    early = jnp.concatenate([w_fio.astype(BF).T, w_out.astype(BF)])
    early = with_layout_constraint(early, Layout((0, 1)))
    early = lax.all_gather(early, ("y", "zh", "zl")).reshape(16, 512, 256)
    x_own, other, idx = lax.optimization_barrier((x_own, other, idx))
    bias = jnp.stack([small[0], other[256]])
    gain = jnp.stack([small[1], other[257]])
    dst = jnp.stack([ds_keep, other[:256]]).reshape(2, 2, 128, 128)

    x_before, x_ahead = shift(x_own, "x", 1), shift(x_own, "x", -1)
    x_ahead, bias, gain, dst = lax.optimization_barrier((x_ahead, bias, gain, dst))
    x_mid = swap(jnp.stack([x_own, x_ahead, x_before]), "c")
    xs = [x_own, x_ahead, shift(x_before[:1], "x", 1), shift(x_ahead[1:], "x", -1), x_before]
    xp = [x_mid, swap(xs[2], "c"), swap(xs[3], "c")]
    wo2 = swap(early[:, 384:], "c")
    late = jnp.concatenate([w_gu.astype(BF).T, w_down.astype(BF)])
    late = after(late, early, *xp)
    late = lax.all_gather(late, ("y", "zh", "zl")).reshape(16, 1056, 256)

    ho, hs, mine, sent = mix_call(idx, xs, xp, early, bias, gain, dst)
    hr = swap(hs, "c")
    other = swap(sent, "zl")
    decode_next = jnp.where(
        zl == 0,
        jnp.concatenate([mine[:2], other[:2]]),
        jnp.concatenate([other[:2], mine[:2]]),
    ).reshape(4, 1, 128, 128)
    prompt_states = jnp.where(
        zl == 0, jnp.stack([mine[2], other[2]]), jnp.stack([other[2], mine[2]])
    ).reshape(2, 1, 128, 128)

    far = out_call((2,), idx, ho, hr, early, wo2)
    rest = out_call((1, 3, 0), idx, after(ho, *far), hr, early, wo2)
    attention = reduce_parts(far, rest, other)
    residual = (x_own.astype(F32) + attention).astype(BF)
    rs = ring_gather(residual, "x")
    late2 = swap(after(late, rs[1], rs[4]), "c")
    hid, *far = mlp_call(idx, rs, late, late2, mlp_gain.reshape(1, 2048))
    down = reduce_parts(far, down_call((1, 3, 0), idx, hid, late, late2))
    layer = (residual.astype(F32) + down).astype(BF)
    layer = layer.reshape(2, HALF, 2, 128).transpose(0, 2, 1, 3).reshape(4, HALF, 128)
    back = lax.all_to_all(layer, ("zl", "c"), 0, 0, tiled=True)
    prompt_out = back[:, :512].reshape(2, 1024, 128)
    decode_out = back[:, 512]
    return (prompt_out, decode_out, prompt_states, decode_next)


def solution(mesh):
    wide = Mesh(mesh.devices.reshape(tuple(SIZES.values())), tuple(SIZES))
    req = ("y", "zh")
    mlp = ("zl", "x", "c")
    return jax.shard_map(
        on_device,
        mesh=wide,
        in_specs=(
            P(req, None, mlp),
            P(req, mlp),
            P(req),
            P(req, mlp, None, None),
            P(req, mlp),
            P(mlp),
            P(mlp),
            P(mlp, req),
            P(),
            P(req, mlp),
            P(mlp, req),
        ),
        out_specs=(
            P(req, None, mlp),
            P(req, mlp),
            P(req, mlp, None, None),
            P(req, mlp, None, None),
        ),
        check_vma=False,
    )
```

```python
import functools

import jax
import jax.numpy as jnp
import numpy as np
from jax import lax
from jax.experimental import pallas as pl
from jax.experimental.layout import Layout, with_layout_constraint
from jax.experimental.pallas import tpu as pltpu
from jax.sharding import Mesh, PartitionSpec as P

EPS = 1e-5
HALF = 528
CH = 128
LEVELS = 7
BF = jnp.bfloat16
F32 = jnp.float32
SIZES = {"y": 4, "zh": 2, "zl": 2, "x": 4, "c": 2}
VMEM_LIMIT = 60 * 1024 * 1024


def shift(value, axis, step):
    n = SIZES[axis]
    return lax.ppermute(value, axis, [(i, (i + step) % n) for i in range(n)])


def ring_gather(own, axis):
    n = own.shape[0] // 2
    before = shift(own, axis, 1)
    ahead = shift(own, axis, -1)
    far0 = shift(before[:n], axis, 1)
    far1 = shift(ahead[n:], axis, -1)
    return [own, ahead, far0, far1, before]


def piece(refs, step, part):
    if step == 2:
        return refs[2 + part].at[0]
    return refs[{0: 0, 1: 1, 3: 4}[step]].at[part]


def level_matrix():
    t = np.arange(CH)[:, None]
    u = np.arange(CH)[None, :]
    rows = []
    for level in range(LEVELS):
        b = 1 << level
        ref = (t // (2 * b)) * 2 * b + b - 1
        late = (t % (2 * b)) >= b
        rows.append(np.where(late, (u > ref) & (u <= t), (u > t) & (u <= ref)))
    rows.append(u <= t)
    rows.append(u > t)
    return np.concatenate(rows, 0).astype(np.float32)


def dot_nt(a, b):
    return lax.dot_general(a, b, (((1,), (1,)), ((), ())), preferred_element_type=F32)


def dot_tn(a, b):
    return lax.dot_general(a, b, (((0,), (0,)), ((), ())), preferred_element_type=F32)


def dot_nn(a, b):
    return jnp.dot(a, b, preferred_element_type=F32)


def copy_all(copies, sems):
    started = []
    for i, (src, dst) in enumerate(copies):
        cp = pltpu.make_async_copy(src, dst, sems.at[i])
        cp.start()
        started.append(cp)
    return started


def col(r):
    return pl.ds(pl.multiple_of(r * 256, 256), 256)


def x_copies(refs, cat, x):
    out = []
    for k in range(4):
        for z in range(2):
            r = z * 4 + ((x + k) & 3)
            out.append((piece(refs, k, z), cat.at[:, col(r)]))
    return out


def head_out(o, gain):
    ms = jnp.mean(o * o, axis=-1, keepdims=True)
    return o * lax.rsqrt(ms + EPS) * gain


def mix_kernel(
    idx, xo0, xo1, xo2, xo3, xo4, xpm, xp2, xp3, w_ref,
    bias_ref, gain_ref, mat_ref, dst_ref,
    own_ref, other_ref, keep_ref, send_ref,
    xcat, wcat, mix, oscr, carry, sems,
):
    x, c, length = idx[3], idx[4], idx[5]
    copies = x_copies((xo0, xo1, xo2, xo3, xo4), xcat.at[0:HALF], x)
    copies += x_copies((xpm.at[0], xpm.at[1], xp2, xp3, xpm.at[2]), xcat.at[HALF : 2 * HALF], x)
    for i in range(16):
        at = pl.multiple_of(((i & 1) ^ idx[2]) * 384, 128)
        r = i // 2
        copies.append((w_ref.at[i, 0:384], wcat.at[pl.ds(at, 384), r * 256 : (r + 1) * 256]))
    for cp in copy_all(copies, sems):
        cp.wait()

    def project(i, unused):
        part = dot_nt(xcat[...], wcat[pl.ds(pl.multiple_of(i * 256, 256), 256), :])
        mix[c, :, col(i)] = part[:HALF]
        mix[1 - c, :, col(i)] = part[HALF:]
        return unused

    lax.fori_loop(0, 3, project, 0)
    carry[...] = jnp.zeros_like(carry)
    t = lax.broadcasted_iota(jnp.int32, (CH, CH), 0)
    s = lax.broadcasted_iota(jnp.int32, (CH, CH), 1)
    pair = jnp.where(t > s, t ^ s, 0)
    diag = t == s
    row = lax.broadcasted_iota(jnp.int32, (CH, 128), 0)

    def chunk(n, unused):
        h = n // 4
        rows = pl.ds(pl.multiple_of((n % 4) * CH, CH), CH)
        alive = (row + n * CH) < length
        for j in range(2):
            z = mix[h, rows, j * 384 : j * 384 + 128] + bias_ref[j : j + 1, :]
            v = mix[h, rows, j * 384 + 128 : j * 384 + 256].astype(BF)
            q = mix[h, rows, j * 384 + 256 : j * 384 + 384]
            e = jnp.exp(-jnp.abs(z))
            logf = jnp.where(alive, jnp.minimum(z, 0.0) - jnp.log1p(e), 0.0)
            inv = 1.0 / (1.0 + e)
            k = jnp.where(alive, jnp.where(z >= 0, e * inv, inv), 0.0)
            hi = logf.astype(BF)
            lo = (logf - hi.astype(F32)).astype(BF)
            d = dot_nn(mat_ref[...], jnp.concatenate([hi, lo], axis=1))
            decay = jnp.exp(d[:, :128] + d[:, 128:])
            scores = jnp.where(diag, dot_nt(q.astype(BF), k.astype(BF)), 0.0)
            for level in range(LEVELS):
                el = decay[level * CH : (level + 1) * CH]
                part = dot_nt((q * el).astype(BF), (k * el).astype(BF))
                scores = jnp.where((pair >> level) == 1, part, scores)
            es = decay[LEVELS * CH : (LEVELS + 1) * CH]
            ee = decay[(LEVELS + 1) * CH :]
            held = carry[j]
            o = dot_nn(scores.astype(BF), v) + dot_nt((q * es).astype(BF), held.astype(BF))
            o = jnp.where(alive, o, 0.0)
            carry[j] = held * es[CH - 1 :, :] + dot_tn(v, (k * ee).astype(BF))
            oscr[h, rows, j * 128 : (j + 1) * 128] = head_out(o, gain_ref[j : j + 1, :]).astype(BF)
        return unused

    lax.fori_loop(0, 8, chunk, 0, unroll=2)
    first = lax.broadcasted_iota(jnp.int32, (16, 128), 0) == 0
    for h in range(2):
        for j in range(2):
            z = mix[h, 512:513, j * 384 : j * 384 + 128] + bias_ref[j : j + 1, :]
            v = mix[h, 512:513, j * 384 + 128 : j * 384 + 256]
            q = mix[h, 512:513, j * 384 + 256 : j * 384 + 384]
            e = jnp.exp(-jnp.abs(z))
            inv = 1.0 / (1.0 + e)
            f = jnp.where(z >= 0, inv, e * inv)
            k = jnp.where(z >= 0, e * inv, inv)
            ft = jnp.broadcast_to(f, (128, 128)).T
            kt = jnp.broadcast_to(k, (128, 128)).T
            qt = jnp.broadcast_to(q, (128, 128)).T
            nxt = ft * dst_ref[j, h] + kt * v
            (keep_ref, send_ref)[j][h] = nxt
            o = head_out(jnp.sum(nxt * qt, axis=0, keepdims=True), gain_ref[j : j + 1, :])
            wide = jnp.where(first, jnp.broadcast_to(o, (16, 128)), 0.0)
            oscr[h, 512:528, j * 128 : (j + 1) * 128] = wide.astype(BF)
    for j in range(2):
        (keep_ref, send_ref)[j][2] = carry[j].T
    own_ref[...] = oscr[c]
    other_ref[...] = oscr[1 - c]


def anyspec():
    return pl.BlockSpec(memory_space=pl.ANY)


def vspec():
    return pl.BlockSpec(memory_space=pltpu.VMEM)


def sspec():
    return pl.BlockSpec(memory_space=pltpu.SMEM)


def cost(us):
    return pl.CostEstimate(flops=us, transcendentals=0, bytes_accessed=us)


def mix_call(idx, xo, xp, w, bias, gain, dst):
    mat = jnp.asarray(level_matrix(), BF)
    return pl.pallas_call(
        mix_kernel,
        out_shape=(
            jax.ShapeDtypeStruct((HALF, 256), BF),
            jax.ShapeDtypeStruct((HALF, 256), BF),
            jax.ShapeDtypeStruct((3, 128, 128), F32),
            jax.ShapeDtypeStruct((3, 128, 128), F32),
        ),
        in_specs=[sspec()] + [anyspec()] * 9 + [vspec()] * 4,
        out_specs=(vspec(),) * 4,
        scratch_shapes=[
            pltpu.VMEM((2 * HALF, 2048), BF),
            pltpu.VMEM((768, 2048), BF),
            pltpu.VMEM((2, HALF, 768), F32),
            pltpu.VMEM((2, HALF, 256), BF),
            pltpu.VMEM((2, 128, 128), F32),
            pltpu.SemaphoreType.DMA((32,)),
        ],
        compiler_params=pltpu.CompilerParams(vmem_limit_bytes=VMEM_LIMIT),
        cost_estimate=cost(24),
        name="mix",
    )(idx, *xo, *xp, w, bias, gain, mat, dst)


PART = jax.ShapeDtypeStruct((2, HALF, 256), F32)
FAR = jax.ShapeDtypeStruct((1, HALF, 256), BF)


def shapes_of(steps):
    return (FAR, FAR) if steps == (2,) else (PART,) * len(steps)


def put(steps, outs, s, z, value):
    if steps == (2,):
        outs[z][0] = value.astype(BF)
    else:
        outs[s][z] = value


def blocks_of(steps, x):
    for s, k in enumerate(steps):
        for z in range(2):
            yield s * 2 + z, s, z, z * 4 + ((x + k) & 3)


def out_kernel(steps, idx, a_ref, b_ref, u_ref, v_ref, *rest):
    outs, (ocat, wcat, sems) = rest[:-3], rest[-3:]
    copies = [(a_ref, ocat.at[:, 0:256]), (b_ref, ocat.at[:, 256:512])]
    for slot, s, z, r in blocks_of(steps, idx[3]):
        for j in range(2):
            for cc in range(2):
                src = v_ref.at[2 * r + j] if cc else u_ref.at[2 * r + j, 384:512]
                at = pl.multiple_of(cc * 256 + (j ^ idx[2]) * 128, 128)
                copies.append((src, wcat.at[slot, pl.ds(at, 128), :]))
    for cp in copy_all(copies, sems):
        cp.wait()
    for slot, s, z, r in blocks_of(steps, idx[3]):
        put(steps, outs, s, z, dot_nn(ocat[...], wcat[slot]))


def out_call(steps, idx, a, b, u, v):
    n = len(steps)
    return pl.pallas_call(
        functools.partial(out_kernel, steps),
        out_shape=shapes_of(steps),
        in_specs=[sspec()] + [anyspec()] * 4,
        out_specs=(vspec(),) * len(shapes_of(steps)),
        scratch_shapes=[
            pltpu.VMEM((HALF, 512), BF),
            pltpu.VMEM((2 * n, 512, 256), BF),
            pltpu.SemaphoreType.DMA((2 + 8 * n,)),
        ],
        compiler_params=pltpu.CompilerParams(vmem_limit_bytes=VMEM_LIMIT),
        cost_estimate=cost(2 * n),
        name="outp",
    )(idx, a, b, u, v)


def down_copies(steps, x, ref, wd):
    out = []
    for slot, s, z, r in blocks_of(steps, x):
        for j in range(2):
            for cc in range(2):
                at = cc * 704 + j * 352
                out.append((ref.at[2 * r + j, cc, 704:1056], wd.at[slot, at : at + 352, :]))
    return out


def down_dots(steps, x, hid, wd, outs):
    for slot, s, z, r in blocks_of(steps, x):
        total = dot_nn(hid[0], wd[slot, 0:704, :]) + dot_nn(hid[1], wd[slot, 704:1408, :])
        put(steps, outs, s, z, total)


def mlp_kernel(idx, x0, x1, x2, x3, x4, w_ref, gain_ref, hid, q0, q1, xcat, wg, wd, sems):
    x = idx[3]
    started = [copy_all(x_copies((x0, x1, x2, x3, x4), xcat, x), sems)]
    for cc in range(2):
        copies = []
        for i in range(16):
            for g in range(2):
                at, r = (i & 1) * 352, i // 2
                dst = wg.at[cc, g, at : at + 352, r * 256 : (r + 1) * 256]
                copies.append((w_ref.at[i, cc, g * 352 : (g + 1) * 352], dst))
        started.append(copy_all(copies, sems.at[8 + cc * 32 : 40 + cc * 32]))
    last = copy_all(down_copies((2,), x, w_ref, wd), sems.at[72:80])
    for cp in started[0]:
        cp.wait()

    def normalize(i, unused):
        rows = pl.ds(pl.multiple_of(i * 48, 16), 48)
        r = xcat[rows, :].astype(F32)
        ms = jnp.mean(r * r, axis=-1, keepdims=True)
        xcat[rows, :] = (r * lax.rsqrt(ms + EPS) * gain_ref[...]).astype(BF)
        return unused

    lax.fori_loop(0, 11, normalize, 0)
    for cc in range(2):
        for cp in started[1 + cc]:
            cp.wait()
        gate = dot_nt(xcat[...], wg[cc, 0])
        up = dot_nt(xcat[...], wg[cc, 1])
        hid[cc] = (gate / (1.0 + jnp.exp(-gate)) * up).astype(BF)
    for cp in last:
        cp.wait()
    down_dots((2,), x, hid, wd, (q0, q1))


def mlp_call(idx, xs, w, gain):
    return pl.pallas_call(
        mlp_kernel,
        out_shape=(jax.ShapeDtypeStruct((2, HALF, 704), BF), FAR, FAR),
        in_specs=[sspec()] + [anyspec()] * 6 + [vspec()],
        out_specs=(vspec(),) * 3,
        scratch_shapes=[
            pltpu.VMEM((HALF, 2048), BF),
            pltpu.VMEM((2, 2, 704, 2048), BF),
            pltpu.VMEM((2, 1408, 256), BF),
            pltpu.SemaphoreType.DMA((80,)),
        ],
        compiler_params=pltpu.CompilerParams(vmem_limit_bytes=VMEM_LIMIT),
        cost_estimate=cost(16),
        name="mlp",
    )(idx, *xs, w, gain)


def down_kernel(steps, idx, hid, w_ref, p0, p1, p2, wd, sems):
    for cp in copy_all(down_copies(steps, idx[3], w_ref, wd), sems):
        cp.wait()
    down_dots(steps, idx[3], hid, wd, (p0, p1, p2))


def down_call(steps, idx, hid, w):
    n = len(steps)
    return pl.pallas_call(
        functools.partial(down_kernel, steps),
        out_shape=shapes_of(steps),
        in_specs=[sspec(), vspec(), anyspec()],
        out_specs=(vspec(),) * n,
        scratch_shapes=[
            pltpu.VMEM((2 * n, 1408, 256), BF),
            pltpu.SemaphoreType.DMA((8 * n,)),
        ],
        compiler_params=pltpu.CompilerParams(vmem_limit_bytes=VMEM_LIMIT),
        cost_estimate=cost(5),
        name="down",
    )(idx, hid, w)


def swap(value, axis):
    return shift(value, axis, 1)


def after(value, *others):
    return lax.optimization_barrier((value,) + others)[0]


def reduce_parts(far, rest, *others):
    p1, p3, p0 = rest
    a, b = shift(far[0], "x", 1), shift(far[1], "x", -1)
    a, b = lax.optimization_barrier((a, b))
    keep = (0, 0, 0)
    p1 = (p1 + lax.pad(a.astype(F32), F32(0), ((0, 1, 0), keep, keep))).astype(BF)
    p3 = (p3 + lax.pad(b.astype(F32), F32(0), ((1, 0, 0), keep, keep))).astype(BF)
    r1 = shift(p1, "x", 1)
    r3 = shift(p3, "x", -1)
    r1 = after(r1, r3, *others)
    return p0 + r1.astype(F32) + r3.astype(F32)


def on_device(
    prompt_tokens, decode_tokens, prompt_lengths, decode_states, w_fio, forget_bias,
    head_gain, w_out, mlp_gain, w_gu, w_down,
):
    ax = {name: lax.axis_index(name) for name in SIZES}
    zl = ax["zl"]
    length = jnp.where(zl == 0, prompt_lengths[0], prompt_lengths[1])
    idx = jnp.stack([ax["y"], ax["zh"], zl, ax["x"], ax["c"], length]).astype(jnp.int32)

    rows = jnp.concatenate(
        [
            prompt_tokens.reshape(2, 2, 512, 128),
            decode_tokens.reshape(2, 2, 1, 128),
            jnp.zeros((2, 2, HALF - 513, 128), BF),
        ],
        axis=2,
    ).reshape(4, HALF, 128)
    got = lax.all_to_all(rows, ("zl", "c"), 0, 0, tiled=True)
    x_own = got.reshape(2, 2, HALF, 128).transpose(0, 2, 1, 3).reshape(2, HALF, 256)

    small = jnp.stack([forget_bias, head_gain])
    ds = decode_states.reshape(2, 256, 128)
    ds_keep = jnp.where(zl == 0, ds[0], ds[1])
    ds_send = jnp.where(zl == 0, ds[1], ds[0])
    other = swap(jnp.concatenate([ds_send, small]), "zl")
    early = jnp.concatenate([w_fio.astype(BF).T, w_out.astype(BF)])
    early = with_layout_constraint(early, Layout((0, 1)))
    early = lax.all_gather(early, ("y", "zh", "zl")).reshape(16, 512, 256)
    x_own, other, idx = lax.optimization_barrier((x_own, other, idx))
    bias = jnp.stack([small[0], other[256]])
    gain = jnp.stack([small[1], other[257]])
    dst = jnp.stack([ds_keep, other[:256]]).reshape(2, 2, 128, 128)

    x_before, x_ahead = shift(x_own, "x", 1), shift(x_own, "x", -1)
    x_ahead, bias, gain, dst = lax.optimization_barrier((x_ahead, bias, gain, dst))
    x_mid = swap(jnp.stack([x_own, x_ahead, x_before]), "c")
    xs = [x_own, x_ahead, shift(x_before[:1], "x", 1), shift(x_ahead[1:], "x", -1), x_before]
    xp = [x_mid, swap(xs[2], "c"), swap(xs[3], "c")]
    wo2 = swap(early[:, 384:], "c")
    late = jnp.concatenate([w_gu.astype(BF).T, w_down.astype(BF)])
    late = after(late, early, *xp)
    late = lax.all_gather(late, ("y", "zh", "zl", "c")).reshape(16, 2, 1056, 256)

    ho, hs, mine, sent = mix_call(idx, xs, xp, early, bias, gain, dst)
    hr = swap(hs, "c")
    other = swap(sent, "zl")
    decode_next = jnp.where(
        zl == 0,
        jnp.concatenate([mine[:2], other[:2]]),
        jnp.concatenate([other[:2], mine[:2]]),
    ).reshape(4, 1, 128, 128)
    prompt_states = jnp.where(
        zl == 0, jnp.stack([mine[2], other[2]]), jnp.stack([other[2], mine[2]])
    ).reshape(2, 1, 128, 128)

    far = out_call((2,), idx, ho, hr, early, wo2)
    rest = out_call((1, 3, 0), idx, after(ho, *far), hr, early, wo2)
    attention = reduce_parts(far, rest, other)
    residual = (x_own.astype(F32) + attention).astype(BF)
    rs = ring_gather(residual, "x")
    hid, *far = mlp_call(idx, rs, late, mlp_gain.reshape(1, 2048))
    down = reduce_parts(far, down_call((1, 3, 0), idx, hid, late))
    layer = (residual.astype(F32) + down).astype(BF)
    layer = layer.reshape(2, HALF, 2, 128).transpose(0, 2, 1, 3).reshape(4, HALF, 128)
    back = lax.all_to_all(layer, ("zl", "c"), 0, 0, tiled=True)
    prompt_out = back[:, :512].reshape(2, 1024, 128)
    decode_out = back[:, 512]
    return (prompt_out, decode_out, prompt_states, decode_next)


def solution(mesh):
    wide = Mesh(mesh.devices.reshape(tuple(SIZES.values())), tuple(SIZES))
    req = ("y", "zh")
    mlp = ("zl", "x", "c")
    return jax.shard_map(
        on_device,
        mesh=wide,
        in_specs=(
            P(req, None, mlp),
            P(req, mlp),
            P(req),
            P(req, mlp, None, None),
            P(req, mlp),
            P(mlp),
            P(mlp),
            P(mlp, req),
            P(),
            P(req, mlp),
            P(mlp, req),
        ),
        out_specs=(
            P(req, None, mlp),
            P(req, mlp),
            P(req, mlp, None, None),
            P(req, mlp, None, None),
        ),
        check_vma=False,
    )
```

```python
import functools

import jax
import jax.numpy as jnp
import numpy as np
from jax import lax
from jax.experimental import pallas as pl
from jax.experimental.layout import Layout, with_layout_constraint
from jax.experimental.pallas import tpu as pltpu
from jax.sharding import Mesh, PartitionSpec as P

EPS = 1e-5
HALF = 528
CH = 128
LEVELS = 7
BF = jnp.bfloat16
F32 = jnp.float32
SIZES = {"y": 4, "zh": 2, "zl": 2, "x": 4, "c": 2}
VMEM_LIMIT = 60 * 1024 * 1024


def shift(value, axis, step):
    n = SIZES[axis]
    return lax.ppermute(value, axis, [(i, (i + step) % n) for i in range(n)])


def ring_gather(own, axis):
    n = own.shape[0] // 2
    before = shift(own, axis, 1)
    ahead = shift(own, axis, -1)
    far0 = shift(before[:n], axis, 1)
    far1 = shift(ahead[n:], axis, -1)
    return [own, ahead, far0, far1, before]


def piece(refs, step, part):
    if step == 2:
        return refs[2 + part].at[0]
    return refs[{0: 0, 1: 1, 3: 4}[step]].at[part]


def level_matrix():
    t = np.arange(CH)[:, None]
    u = np.arange(CH)[None, :]
    rows = []
    for level in range(LEVELS):
        b = 1 << level
        ref = (t // (2 * b)) * 2 * b + b - 1
        late = (t % (2 * b)) >= b
        rows.append(np.where(late, (u > ref) & (u <= t), (u > t) & (u <= ref)))
    rows.append(u <= t)
    rows.append(u > t)
    return np.concatenate(rows, 0).astype(np.float32)


def dot_nt(a, b):
    return lax.dot_general(a, b, (((1,), (1,)), ((), ())), preferred_element_type=F32)


def dot_tn(a, b):
    return lax.dot_general(a, b, (((0,), (0,)), ((), ())), preferred_element_type=F32)


def dot_nn(a, b):
    return jnp.dot(a, b, preferred_element_type=F32)


def copy_all(copies, sems):
    started = []
    for i, (src, dst) in enumerate(copies):
        cp = pltpu.make_async_copy(src, dst, sems.at[i])
        cp.start()
        started.append(cp)
    return started


def col(r):
    return pl.ds(pl.multiple_of(r * 256, 256), 256)


def x_copies(refs, cat, x):
    out = []
    for k in range(4):
        for z in range(2):
            r = z * 4 + ((x + k) & 3)
            out.append((piece(refs, k, z), cat.at[:, col(r)]))
    return out


def head_out(o, gain):
    ms = jnp.mean(o * o, axis=-1, keepdims=True)
    return o * lax.rsqrt(ms + EPS) * gain


def mix_kernel(
    idx, xo0, xo1, xo2, xo3, xo4, xpm, xp2, xp3, w_ref,
    bias_ref, gain_ref, mat_ref, dst_ref,
    own_ref, other_ref, keep_ref, send_ref,
    xcat, wcat, mix, oscr, carry, sems,
):
    x, c, length = idx[3], idx[4], idx[5]
    copies = x_copies((xo0, xo1, xo2, xo3, xo4), xcat.at[0:HALF], x)
    copies += x_copies((xpm.at[0], xpm.at[1], xp2, xp3, xpm.at[2]), xcat.at[HALF : 2 * HALF], x)
    for i in range(16):
        at = pl.multiple_of(((i & 1) ^ idx[2]) * 384, 128)
        r = i // 2
        copies.append((w_ref.at[i, 0:384], wcat.at[pl.ds(at, 384), r * 256 : (r + 1) * 256]))
    for cp in copy_all(copies, sems):
        cp.wait()

    def project(i, unused):
        part = dot_nt(xcat[...], wcat[pl.ds(pl.multiple_of(i * 256, 256), 256), :])
        mix[c, :, col(i)] = part[:HALF]
        mix[1 - c, :, col(i)] = part[HALF:]
        return unused

    lax.fori_loop(0, 3, project, 0)
    carry[...] = jnp.zeros_like(carry)
    t = lax.broadcasted_iota(jnp.int32, (CH, CH), 0)
    s = lax.broadcasted_iota(jnp.int32, (CH, CH), 1)
    pair = jnp.where(t > s, t ^ s, 0)
    diag = t == s
    row = lax.broadcasted_iota(jnp.int32, (CH, 128), 0)

    def chunk(n, unused):
        h = n // 4
        rows = pl.ds(pl.multiple_of((n % 4) * CH, CH), CH)
        alive = (row + n * CH) < length
        for j in range(2):
            z = mix[h, rows, j * 384 : j * 384 + 128] + bias_ref[j : j + 1, :]
            v = mix[h, rows, j * 384 + 128 : j * 384 + 256].astype(BF)
            q = mix[h, rows, j * 384 + 256 : j * 384 + 384]
            e = jnp.exp(-jnp.abs(z))
            logf = jnp.where(alive, jnp.minimum(z, 0.0) - jnp.log1p(e), 0.0)
            inv = 1.0 / (1.0 + e)
            k = jnp.where(alive, jnp.where(z >= 0, e * inv, inv), 0.0)
            hi = logf.astype(BF)
            lo = (logf - hi.astype(F32)).astype(BF)
            d = dot_nn(mat_ref[...], jnp.concatenate([hi, lo], axis=1))
            decay = jnp.exp(d[:, :128] + d[:, 128:])
            scores = jnp.where(diag, dot_nt(q.astype(BF), k.astype(BF)), 0.0)
            for level in range(LEVELS):
                el = decay[level * CH : (level + 1) * CH]
                part = dot_nt((q * el).astype(BF), (k * el).astype(BF))
                scores = jnp.where((pair >> level) == 1, part, scores)
            es = decay[LEVELS * CH : (LEVELS + 1) * CH]
            ee = decay[(LEVELS + 1) * CH :]
            held = carry[j]
            o = dot_nn(scores.astype(BF), v) + dot_nt((q * es).astype(BF), held.astype(BF))
            o = jnp.where(alive, o, 0.0)
            carry[j] = held * es[CH - 1 :, :] + dot_tn(v, (k * ee).astype(BF))
            oscr[h, rows, j * 128 : (j + 1) * 128] = head_out(o, gain_ref[j : j + 1, :]).astype(BF)
        return unused

    lax.fori_loop(0, 8, chunk, 0, unroll=2)
    first = lax.broadcasted_iota(jnp.int32, (16, 128), 0) == 0
    for h in range(2):
        for j in range(2):
            z = mix[h, 512:513, j * 384 : j * 384 + 128] + bias_ref[j : j + 1, :]
            v = mix[h, 512:513, j * 384 + 128 : j * 384 + 256]
            q = mix[h, 512:513, j * 384 + 256 : j * 384 + 384]
            e = jnp.exp(-jnp.abs(z))
            inv = 1.0 / (1.0 + e)
            f = jnp.where(z >= 0, inv, e * inv)
            k = jnp.where(z >= 0, e * inv, inv)
            ft = jnp.broadcast_to(f, (128, 128)).T
            kt = jnp.broadcast_to(k, (128, 128)).T
            qt = jnp.broadcast_to(q, (128, 128)).T
            nxt = ft * dst_ref[j, h] + kt * v
            (keep_ref, send_ref)[j][h] = nxt
            o = head_out(jnp.sum(nxt * qt, axis=0, keepdims=True), gain_ref[j : j + 1, :])
            wide = jnp.where(first, jnp.broadcast_to(o, (16, 128)), 0.0)
            oscr[h, 512:528, j * 128 : (j + 1) * 128] = wide.astype(BF)
    for j in range(2):
        (keep_ref, send_ref)[j][2] = carry[j].T
    own_ref[...] = oscr[c]
    other_ref[...] = oscr[1 - c]


def anyspec():
    return pl.BlockSpec(memory_space=pl.ANY)


def vspec():
    return pl.BlockSpec(memory_space=pltpu.VMEM)


def sspec():
    return pl.BlockSpec(memory_space=pltpu.SMEM)


def cost(us):
    return pl.CostEstimate(flops=us, transcendentals=0, bytes_accessed=us)


def mix_call(idx, xo, xp, w, bias, gain, dst):
    mat = jnp.asarray(level_matrix(), BF)
    return pl.pallas_call(
        mix_kernel,
        out_shape=(
            jax.ShapeDtypeStruct((HALF, 256), BF),
            jax.ShapeDtypeStruct((HALF, 256), BF),
            jax.ShapeDtypeStruct((3, 128, 128), F32),
            jax.ShapeDtypeStruct((3, 128, 128), F32),
        ),
        in_specs=[sspec()] + [anyspec()] * 9 + [vspec()] * 4,
        out_specs=(vspec(),) * 4,
        scratch_shapes=[
            pltpu.VMEM((2 * HALF, 2048), BF),
            pltpu.VMEM((768, 2048), BF),
            pltpu.VMEM((2, HALF, 768), F32),
            pltpu.VMEM((2, HALF, 256), BF),
            pltpu.VMEM((2, 128, 128), F32),
            pltpu.SemaphoreType.DMA((32,)),
        ],
        compiler_params=pltpu.CompilerParams(vmem_limit_bytes=VMEM_LIMIT),
        cost_estimate=cost(24),
        name="mix",
    )(idx, *xo, *xp, w, bias, gain, mat, dst)


PART = jax.ShapeDtypeStruct((2, HALF, 256), F32)
FAR = jax.ShapeDtypeStruct((1, HALF, 256), BF)


def shapes_of(steps):
    return (FAR, FAR) if steps == (2,) else (PART,) * len(steps)


def put(steps, outs, s, z, value):
    if steps == (2,):
        outs[z][0] = value.astype(BF)
    else:
        outs[s][z] = value


def blocks_of(steps, x):
    for s, k in enumerate(steps):
        for z in range(2):
            yield s * 2 + z, s, z, z * 4 + ((x + k) & 3)


def out_kernel(steps, idx, a_ref, b_ref, u_ref, v_ref, *rest):
    outs, (ocat, wcat, sems) = rest[:-3], rest[-3:]
    copies = [(a_ref, ocat.at[:, 0:256]), (b_ref, ocat.at[:, 256:512])]
    for slot, s, z, r in blocks_of(steps, idx[3]):
        for j in range(2):
            for cc in range(2):
                src = v_ref.at[2 * r + j] if cc else u_ref.at[2 * r + j, 384:512]
                at = pl.multiple_of(cc * 256 + (j ^ idx[2]) * 128, 128)
                copies.append((src, wcat.at[slot, pl.ds(at, 128), :]))
    for cp in copy_all(copies, sems):
        cp.wait()
    for slot, s, z, r in blocks_of(steps, idx[3]):
        put(steps, outs, s, z, dot_nn(ocat[...], wcat[slot]))


def out_call(steps, idx, a, b, u, v):
    n = len(steps)
    return pl.pallas_call(
        functools.partial(out_kernel, steps),
        out_shape=shapes_of(steps),
        in_specs=[sspec()] + [anyspec()] * 4,
        out_specs=(vspec(),) * len(shapes_of(steps)),
        scratch_shapes=[
            pltpu.VMEM((HALF, 512), BF),
            pltpu.VMEM((2 * n, 512, 256), BF),
            pltpu.SemaphoreType.DMA((2 + 8 * n,)),
        ],
        compiler_params=pltpu.CompilerParams(vmem_limit_bytes=VMEM_LIMIT),
        cost_estimate=cost(2 * n),
        name="outp",
    )(idx, a, b, u, v)


def down_copies(steps, x, ref, wd):
    out = []
    for slot, s, z, r in blocks_of(steps, x):
        for j in range(2):
            for cc in range(2):
                at = cc * 704 + j * 352
                out.append((ref.at[2 * r + j, cc, 704:1056], wd.at[slot, at : at + 352, :]))
    return out


def down_dots(steps, x, hid, wd, outs, started):
    for slot, s, z, r in blocks_of(steps, x):
        for cp in started[slot * 4 : slot * 4 + 4]:
            cp.wait()
        total = dot_nn(hid[0], wd[slot, 0:704, :]) + dot_nn(hid[1], wd[slot, 704:1408, :])
        put(steps, outs, s, z, total)


def mlp_kernel(idx, x0, x1, x2, x3, x4, w_ref, gain_ref, hid, q0, q1, xcat, wg, wd, sems):
    x = idx[3]
    started = [copy_all(x_copies((x0, x1, x2, x3, x4), xcat, x), sems)]
    for cc in range(2):
        copies = []
        for i in range(16):
            for g in range(2):
                at, r = (i & 1) * 352, i // 2
                dst = wg.at[cc, g, at : at + 352, r * 256 : (r + 1) * 256]
                copies.append((w_ref.at[i, cc, g * 352 : (g + 1) * 352], dst))
        started.append(copy_all(copies, sems.at[8 + cc * 32 : 40 + cc * 32]))
    last = copy_all(down_copies((2,), x, w_ref, wd), sems.at[72:80])
    for cp in started[0]:
        cp.wait()

    def normalize(i, unused):
        rows = pl.ds(pl.multiple_of(i * 48, 16), 48)
        r = xcat[rows, :].astype(F32)
        ms = jnp.mean(r * r, axis=-1, keepdims=True)
        xcat[rows, :] = (r * lax.rsqrt(ms + EPS) * gain_ref[...]).astype(BF)
        return unused

    lax.fori_loop(0, 11, normalize, 0)
    for cc in range(2):
        for cp in started[1 + cc]:
            cp.wait()
        gate = dot_nt(xcat[...], wg[cc, 0])
        up = dot_nt(xcat[...], wg[cc, 1])
        hid[cc] = (gate / (1.0 + jnp.exp(-gate)) * up).astype(BF)
    down_dots((2,), x, hid, wd, (q0, q1), last)


def mlp_call(idx, xs, w, gain):
    return pl.pallas_call(
        mlp_kernel,
        out_shape=(jax.ShapeDtypeStruct((2, HALF, 704), BF), FAR, FAR),
        in_specs=[sspec()] + [anyspec()] * 6 + [vspec()],
        out_specs=(vspec(),) * 3,
        scratch_shapes=[
            pltpu.VMEM((HALF, 2048), BF),
            pltpu.VMEM((2, 2, 704, 2048), BF),
            pltpu.VMEM((2, 1408, 256), BF),
            pltpu.SemaphoreType.DMA((80,)),
        ],
        compiler_params=pltpu.CompilerParams(vmem_limit_bytes=VMEM_LIMIT),
        cost_estimate=cost(16),
        name="mlp",
    )(idx, *xs, w, gain)


def down_kernel(steps, idx, hid, w_ref, p0, p1, p2, wd, sems):
    started = copy_all(down_copies(steps, idx[3], w_ref, wd), sems)
    down_dots(steps, idx[3], hid, wd, (p0, p1, p2), started)


def down_call(steps, idx, hid, w):
    n = len(steps)
    return pl.pallas_call(
        functools.partial(down_kernel, steps),
        out_shape=shapes_of(steps),
        in_specs=[sspec(), vspec(), anyspec()],
        out_specs=(vspec(),) * n,
        scratch_shapes=[
            pltpu.VMEM((2 * n, 1408, 256), BF),
            pltpu.SemaphoreType.DMA((8 * n,)),
        ],
        compiler_params=pltpu.CompilerParams(vmem_limit_bytes=VMEM_LIMIT),
        cost_estimate=cost(5),
        name="down",
    )(idx, hid, w)


def swap(value, axis):
    return shift(value, axis, 1)


def after(value, *others):
    return lax.optimization_barrier((value,) + others)[0]


def reduce_parts(far, rest, *others):
    p1, p3, p0 = rest
    a, b = shift(far[0], "x", 1), shift(far[1], "x", -1)
    a, b = lax.optimization_barrier((a, b))
    keep = (0, 0, 0)
    p1 = (p1 + lax.pad(a.astype(F32), F32(0), ((0, 1, 0), keep, keep))).astype(BF)
    p3 = (p3 + lax.pad(b.astype(F32), F32(0), ((1, 0, 0), keep, keep))).astype(BF)
    r1 = shift(p1, "x", 1)
    r3 = shift(p3, "x", -1)
    r1 = after(r1, r3, *others)
    return p0 + r1.astype(F32) + r3.astype(F32)


def on_device(
    prompt_tokens, decode_tokens, prompt_lengths, decode_states, w_fio, forget_bias,
    head_gain, w_out, mlp_gain, w_gu, w_down,
):
    ax = {name: lax.axis_index(name) for name in SIZES}
    zl = ax["zl"]
    length = jnp.where(zl == 0, prompt_lengths[0], prompt_lengths[1])
    idx = jnp.stack([ax["y"], ax["zh"], zl, ax["x"], ax["c"], length]).astype(jnp.int32)

    rows = jnp.concatenate(
        [
            prompt_tokens.reshape(2, 2, 512, 128),
            decode_tokens.reshape(2, 2, 1, 128),
            jnp.zeros((2, 2, HALF - 513, 128), BF),
        ],
        axis=2,
    ).reshape(4, HALF, 128)
    got = lax.all_to_all(rows, ("zl", "c"), 0, 0, tiled=True)
    x_own = got.reshape(2, 2, HALF, 128).transpose(0, 2, 1, 3).reshape(2, HALF, 256)

    small = jnp.stack([forget_bias, head_gain])
    ds = decode_states.reshape(2, 256, 128)
    ds_keep = jnp.where(zl == 0, ds[0], ds[1])
    ds_send = jnp.where(zl == 0, ds[1], ds[0])
    other = swap(jnp.concatenate([ds_send, small]), "zl")
    early = jnp.concatenate([w_fio.astype(BF).T, w_out.astype(BF)])
    early = with_layout_constraint(early, Layout((0, 1)))
    early = lax.all_gather(early, ("y", "zh", "zl")).reshape(16, 512, 256)
    x_own, other, idx = lax.optimization_barrier((x_own, other, idx))
    bias = jnp.stack([small[0], other[256]])
    gain = jnp.stack([small[1], other[257]])
    dst = jnp.stack([ds_keep, other[:256]]).reshape(2, 2, 128, 128)

    x_before, x_ahead = shift(x_own, "x", 1), shift(x_own, "x", -1)
    x_ahead, bias, gain, dst = lax.optimization_barrier((x_ahead, bias, gain, dst))
    x_mid = swap(jnp.stack([x_own, x_ahead, x_before]), "c")
    xs = [x_own, x_ahead, shift(x_before[:1], "x", 1), shift(x_ahead[1:], "x", -1), x_before]
    xp = [x_mid, swap(xs[2], "c"), swap(xs[3], "c")]
    wo2 = swap(early[:, 384:], "c")
    late = jnp.concatenate([w_gu.astype(BF).T, w_down.astype(BF)])
    late = after(late, early, *xp)
    late = lax.all_gather(late, ("y", "zh", "zl", "c")).reshape(16, 2, 1056, 256)

    ho, hs, mine, sent = mix_call(idx, xs, xp, early, bias, gain, dst)
    hr = swap(hs, "c")
    other = swap(sent, "zl")
    decode_next = jnp.where(
        zl == 0,
        jnp.concatenate([mine[:2], other[:2]]),
        jnp.concatenate([other[:2], mine[:2]]),
    ).reshape(4, 1, 128, 128)
    prompt_states = jnp.where(
        zl == 0, jnp.stack([mine[2], other[2]]), jnp.stack([other[2], mine[2]])
    ).reshape(2, 1, 128, 128)

    far = out_call((2,), idx, ho, hr, early, wo2)
    rest = out_call((1, 3, 0), idx, after(ho, *far), hr, early, wo2)
    attention = reduce_parts(far, rest, other)
    residual = (x_own.astype(F32) + attention).astype(BF)
    rs = ring_gather(residual, "x")
    hid, *far = mlp_call(idx, rs, late, mlp_gain.reshape(1, 2048))
    down = reduce_parts(far, down_call((1, 3, 0), idx, hid, late))
    layer = (residual.astype(F32) + down).astype(BF)
    layer = layer.reshape(2, HALF, 2, 128).transpose(0, 2, 1, 3).reshape(4, HALF, 128)
    back = lax.all_to_all(layer, ("zl", "c"), 0, 0, tiled=True)
    prompt_out = back[:, :512].reshape(2, 1024, 128)
    decode_out = back[:, 512]
    return (prompt_out, decode_out, prompt_states, decode_next)


def solution(mesh):
    wide = Mesh(mesh.devices.reshape(tuple(SIZES.values())), tuple(SIZES))
    req = ("y", "zh")
    mlp = ("zl", "x", "c")
    return jax.shard_map(
        on_device,
        mesh=wide,
        in_specs=(
            P(req, None, mlp),
            P(req, mlp),
            P(req),
            P(req, mlp, None, None),
            P(req, mlp),
            P(mlp),
            P(mlp),
            P(mlp, req),
            P(),
            P(req, mlp),
            P(mlp, req),
        ),
        out_specs=(
            P(req, None, mlp),
            P(req, mlp),
            P(req, mlp, None, None),
            P(req, mlp, None, None),
        ),
        check_vma=False,
    )
```
